32 devices in a mesh: pp: 4 (over y, x), cp: 4 (over z), tp: 2 (over core).
Axes of the slice: x: 2, y: 2, z: 4, core: 2. Of those that a mesh axis runs over, the one named last changes fastest.
Arguments:
- queries: bfloat16 [2048, 16384], P(('pp', 'cp'), 'tp'), may hold values from -12 to 12
- keys: bfloat16 [2048, 1024], P(('pp', 'cp'), 'tp'), may hold values from -12 to 12
- values: bfloat16 [2048, 1024], P(('pp', 'cp'), 'tp'), may hold values from -6 to 6
- pair_order: int32 [4, 4], replicated, may hold values from 0 to 3, each once within a row
- lengths: int32 [4, 2], replicated, may hold values from 128 to 256
- routes: int32 [4, 512, 1], P(None, 'cp'), may hold values from 0 to 7; in each aligned block of 128 rows (0 to 127, 128 to 255, ..., all dimensions but the last counted through in order) at most 32 rows name the same one
Outputs:
- rebalanced: bfloat16 [4096, 16384], P(('pp', 'cp', 'tp'))
The draws below stay inside these ranges and needn't reach their ends.
Inputs may be any that keep to these rules, and one draw needn't show every extreme that they name: `routes`: at most 32 rows of one device's block name the same destination, and in some block one destination is named by exactly 32 rows.
All inputs are finite; a program needn't handle non-finite values.
Results may differ from the reference program's by a relative error of at most 0.003.
Values may be sent and summed in bfloat16 or wider, within the bound.
No kernel may reach another device: no remote copies, remote signals or barrier semaphores. Data moves between devices by JAX's collectives and lax.ppermute only.
A program may use at most 64 MiB of HBM per device.

```python
import math
import jax
import jax.numpy as jnp
import numpy as np
from jax import lax

HEADS = 128
KV = 8
HD = 128
CH = 32
TOK_DEV = 128
SEQ = 256
CAP = 32
TOTAL_ROWS = 2048
N_PP = 4
N_CP = 4
N_TP = 2


def paired_fields(key):
    block_count = N_PP * N_CP
    group_size = HEADS // KV
    query_key, keys_key = jax.random.split(key, 2)
    query_shape = (block_count, 2, 2, CH, KV, group_size, HD)
    key_shape = (block_count, 2, 2, CH, KV, HD)
    query_field = 1.5 * jax.random.normal(query_key, query_shape, jnp.float32)
    key_field = 1.5 * jax.random.normal(keys_key, key_shape, jnp.float32)
    query_field = jnp.clip(query_field, -12.0, 12.0).reshape(block_count * 4 * CH, HEADS * HD)
    key_field = jnp.clip(key_field, -12.0, 12.0).reshape(block_count * 4 * CH, KV * HD)
    return (query_field, key_field)


def draw_queries(key, part):
    return paired_fields(jax.random.fold_in(key, 17))[0].astype(jnp.bfloat16)


def draw_keys(key, part):
    return paired_fields(jax.random.fold_in(key, 17))[1].astype(jnp.bfloat16)


def set_ends(entries, rng, smallest, largest):
    longest = entries.shape.index(max(entries.shape))
    spots = []
    for shift in (0, 1):
        where = [jax.random.randint(jax.random.fold_in(rng, axis), (), 0, length) for axis, length in enumerate(entries.shape)]
        where[longest] = (where[longest] + shift) % entries.shape[longest]
        spots.append(tuple(where))
    return entries.at[spots[0]].set(smallest).at[spots[1]].set(largest)


def steps_of(own_key, shape, cuts, smallest, high):
    gain, own = 1.0, jax.random.fold_in(own_key, 6)
    for axis_at, shards_of in cuts:
        draws = jnp.exp(jax.random.uniform(jax.random.fold_in(own, axis_at), (shards_of,), jnp.float32, smallest / len(cuts), high / len(cuts)))
        gain = gain * jnp.repeat(draws, shape[axis_at] // shards_of).reshape([-1 if axis == axis_at else 1 for axis in range(len(shape))])
    return gain


def deal_out(rng, own, number, rows, count, top, most, skew):
    ranking = jax.random.permutation(rng, count)
    heavy_load, ordinary = portions_of(count, rows * top, most, skew, True), portions_of(count, rows * top, most, skew, False)
    places = jnp.arange(count)

    def named(sizes, turn):
        used = int((sizes > 0).sum())
        fixed = max(1, used // 4)
        moved = fixed + (places - fixed + turn * (used - fixed)) % max(1, count - fixed)
        return jnp.zeros((count,), jnp.int32).at[ranking[jnp.where(places < fixed, places, moved)]].set(jnp.asarray(sizes, jnp.int32))

    sizes = jnp.where(number % 4 == 0, named(heavy_load, number // 4), named(ordinary, number - number // 4 - 1))
    mixed = jax.random.permutation(jax.random.fold_in(own, 3), count)
    giver, receiver = mixed[0:count // 2 * 2:2], mixed[1:count // 2 * 2:2]
    margin = jnp.minimum(sizes[giver] - 1, most - sizes[receiver]) // 2
    margin = jnp.where((giver == ranking[0]) | (receiver == ranking[0]) | (sizes[receiver] == 0), 0, jnp.maximum(margin, 0))
    moved = jax.random.randint(jax.random.fold_in(own, 4), (count // 2,), 0, 1 << 20) % (margin + 1)
    sizes = sizes.at[giver].add(-moved).at[receiver].add(moved)
    items = jnp.searchsorted(jnp.cumsum(sizes), jnp.arange(rows * top), side="right").astype(jnp.int32)
    table = items.reshape(top, rows).T
    table = table[jax.random.permutation(jax.random.fold_in(own, 1), rows)]
    turn = jax.random.randint(jax.random.fold_in(own, 2), (rows, 1), 0, top)
    return jnp.take_along_axis(table, (jnp.arange(top)[None, :] + turn) % top, axis=1)


def portions_of(number_of, total, reach, skew, full):
    weights = [(1 << 20) // math.isqrt(standing ** skew) + 1 for standing in range(1, number_of + 1)]
    largest = reach if full else min(reach, max(-(-total // number_of), total * weights[0] // sum(weights)))
    least = 1 if total - largest >= number_of - 1 else 0
    holding, rest = [largest] + [least] * (number_of - 1), total - largest - least * (number_of - 1)
    while rest > 0:
        movable = [i for i in range(1, number_of) if holding[i] < largest] or [i for i in range(1, number_of) if holding[i] < reach]
        pool, budget = sum([weights[i] for i in movable]), rest
        for i in movable:
            addition = min(reach - holding[i], max(1, budget * weights[i] // pool), rest)
            holding[i] = holding[i] + addition
            rest = rest - addition
    return np.array(holding)


def centred(own_key, shape, scale, most, shards=(), kind=jnp.bfloat16):
    result = jax.random.normal(own_key, shape, jnp.float32) * scale
    if len(shards) > 0:
        result = steps_of(own_key, shape, shards, -0.22, 0.18) * result
    return jnp.clip(result, min=-most, max=most).astype(kind)


def setup_inputs(seed: int = 0) -> dict:
    key_list = jax.random.split(jax.random.key(seed), 7)
    queries = draw_queries(jax.random.fold_in(key_list[6], 71), 0)
    keys = draw_keys(jax.random.fold_in(key_list[6], 71), 0)
    values = centred(key_list[2], (TOTAL_ROWS, KV * HD), 1.0, 6.0, ((0, 16), (1, 2)))
    pair_order = jax.vmap(lambda own: jax.random.permutation(own, N_CP))(jax.random.split(key_list[3], N_PP)).reshape((N_PP, N_CP)).astype(jnp.int32)
    lengths = set_ends(jax.random.randint(key_list[4], (N_PP, 2), SEQ // 2, SEQ + 1), jax.random.fold_in(key_list[4], 1), SEQ // 2, SEQ).astype(jnp.int32)
    routes_keys = jax.random.split(jax.random.fold_in(key_list[5], 1), N_PP * (N_CP * TOK_DEV) // TOK_DEV)
    routes_turns = jax.random.permutation(jax.random.fold_in(key_list[5], 3), N_PP * (N_CP * TOK_DEV) // TOK_DEV)
    routes = jax.vmap(lambda own, number: deal_out(jax.random.fold_in(key_list[5], 2), own, number, TOK_DEV, N_CP * N_TP, 1, CAP, 1))(routes_keys, routes_turns).reshape((N_PP, N_CP * TOK_DEV, 1))
    return {"queries": queries, "keys": keys, "values": values, "pair_order": pair_order, "lengths": lengths, "routes": routes}


masked_score = -1e30


def pair_positions(pair_ids):
    offsets = jnp.arange(CH, dtype=jnp.int32)
    first_half = pair_ids[:, None] * CH + offsets[None, :]
    second_half = (2 * N_CP - 1 - pair_ids)[:, None] * CH + offsets[None, :]
    return jnp.concatenate([first_half, second_half], axis=1).reshape(-1)


def group_attention(query_group, key_group, value_group, positions, limit):
    scores = jnp.einsum("qrd,kd->rqk", query_group.astype(jnp.float32), key_group.astype(jnp.float32)) * (HD ** -0.5)
    allowed = jnp.logical_and(positions[None, :] <= positions[:, None], positions[None, :] < limit)
    row_max = jnp.max(jnp.where(allowed[None], scores, masked_score), axis=2, keepdims=True)
    weights = jnp.where(allowed[None], jnp.exp(scores - row_max), 0.0)
    total = jnp.sum(weights, axis=2)
    rounded = lax.optimization_barrier(weights.astype(jnp.bfloat16)).astype(jnp.float32)
    summed = jnp.einsum("rqk,kd->qrd", rounded, value_group.astype(jnp.float32))
    return (summed / jnp.transpose(total)[:, :, None]).astype(jnp.bfloat16)


def reference(queries, keys, values, pair_order, lengths, routes):
    group_size = HEADS // KV
    section_rows = N_CP * TOK_DEV
    dest_count = N_CP * N_TP
    width = HEADS * HD
    sections = []
    for section in range(N_PP):
        low_row = section * section_rows
        query_part = queries[low_row:low_row + section_rows].reshape(N_CP, 2, 2 * CH, KV, group_size, HD)
        query_part = jnp.transpose(query_part, (1, 0, 2, 3, 4, 5)).reshape(2, N_CP * 2 * CH, KV, group_size, HD)
        key_part = keys[low_row:low_row + section_rows].reshape(N_CP, 2, 2 * CH, KV, HD)
        key_part = jnp.transpose(key_part, (1, 0, 2, 3, 4)).reshape(2, N_CP * 2 * CH, KV, HD)
        value_part = values[low_row:low_row + section_rows].reshape(N_CP, 2, 2 * CH, KV, HD)
        value_part = jnp.transpose(value_part, (1, 0, 2, 3, 4)).reshape(2, N_CP * 2 * CH, KV, HD)
        positions = pair_positions(pair_order[section])
        outcome = []
        for sequence in range(2):
            limit = lengths[section, sequence]

            def per_group(operands):
                return group_attention(operands[0], operands[1], operands[2], positions, limit)

            grouped = lax.map(per_group, (jnp.moveaxis(query_part[sequence], 1, 0), jnp.moveaxis(key_part[sequence], 1, 0), jnp.moveaxis(value_part[sequence], 1, 0)))
            outcome.append(jnp.moveaxis(grouped, 0, 1))
        attended = jnp.stack(outcome).reshape(2, N_CP, 2 * CH, width)
        attended = jnp.transpose(attended, (1, 0, 2, 3)).reshape(N_CP * TOK_DEV, width)
        targets = routes[section, :, 0].reshape(N_CP, TOK_DEV)
        matches = (targets[:, :, None] == jnp.arange(dest_count, dtype=jnp.int32)[None, None, :]).astype(jnp.int32)
        counts = jnp.cumsum(matches, axis=1) - matches
        slot_index = jnp.sum(matches * counts, axis=2)
        place_index = targets * (N_CP * CAP) + jnp.arange(N_CP, dtype=jnp.int32)[:, None] * CAP + slot_index
        arranged = jnp.zeros((dest_count * N_CP * CAP, width), jnp.bfloat16)
        arranged = arranged.at[place_index.reshape(-1)].set(attended)
        sections.append(arranged)
    return jnp.concatenate([sections[(target_segment + N_PP - 1) % N_PP] for target_segment in range(N_PP)], axis=0)
```

```python
import jax
import jax.numpy as jnp
from jax import lax
from jax.experimental import pallas as pl
from jax.experimental.pallas import tpu as pltpu
from jax.sharding import PartitionSpec as P

HD = 128


masked_score = -1e30


def shifted(block, axis, distance):
    devices = range(lax.axis_size(axis))
    route = [((i - distance) % len(devices), i) for i in devices]
    return lax.ppermute(block, axis, route)


def pair_positions(pair_ids, block_len, cycle_size):
    offsets = jnp.arange(block_len, dtype=jnp.int32)
    first_half = pair_ids[:, None] * block_len + offsets[None, :]
    second_half = (2 * cycle_size - 1 - pair_ids)[:, None] * block_len + offsets[None, :]
    return jnp.concatenate([first_half, second_half], axis=1)


def dispatch_rows(attended, targets, dest_count, capacity):
    row_count = attended.shape[0]
    matches = targets[:, None] == jnp.arange(dest_count, dtype=jnp.int32)[None, :]
    row_ids = jnp.arange(row_count, dtype=jnp.int32)
    earlier = (row_ids[None, :] < row_ids[:, None]).astype(jnp.bfloat16)
    before = jnp.dot(earlier, matches.astype(jnp.bfloat16), preferred_element_type=jnp.float32)
    slot_index = jnp.sum(jnp.where(matches, before, 0.0), axis=1).astype(jnp.int32)
    slot_ids = jnp.arange(capacity, dtype=jnp.int32)
    picked_rows = jnp.logical_and(
        jnp.transpose(matches)[:, None, :], slot_index[None, None, :] == slot_ids[None, :, None]
    )
    selector = picked_rows.astype(jnp.bfloat16).reshape(dest_count * capacity, row_count)
    return jnp.dot(selector, attended, preferred_element_type=jnp.float32).astype(jnp.bfloat16)


def spread_rows(buffer, cycle_size, split_size, capacity, width):
    flat_buffer = buffer.reshape(cycle_size * split_size, capacity, width)
    moved = lax.all_to_all(flat_buffer, ("cp", "tp"), split_axis=0, concat_axis=0, tiled=True)
    moved = jnp.transpose(moved.reshape(cycle_size, split_size, capacity, width), (0, 2, 1, 3))
    return moved.reshape(cycle_size * capacity, split_size * width)


def arrange_rows(attended, routes, source, cycle_size, split_size):
    row_count, width = attended.shape
    dest_count = cycle_size * split_size
    capacity = 2 * row_count // dest_count
    targets = lax.dynamic_index_in_dim(routes, source, 0, keepdims=False)[:, 0]
    buffer = dispatch_rows(attended, targets, dest_count, capacity)
    buffer = buffer.reshape(cycle_size, split_size, capacity, width)
    return spread_rows(buffer, cycle_size, split_size, capacity, width)


def general_body(queries, keys, values, pair_order, lengths, routes):
    cycle_size = lax.axis_size("cp")
    split_size = lax.axis_size("tp")
    section = lax.axis_index("pp")
    place = lax.axis_index("cp")
    row_count = queries.shape[0]
    block_len = row_count // 4
    width = queries.shape[1]
    group_count = keys.shape[1] // HD
    group_size = width // keys.shape[1]
    score_scale = HD ** (-0.5)
    order_row = lax.dynamic_index_in_dim(pair_order, section, 0, keepdims=False)
    own_pair = lax.dynamic_index_in_dim(order_row, place, 0, keepdims=True)
    query_pos = pair_positions(own_pair, block_len, cycle_size).reshape(2 * block_len)
    limits = lax.dynamic_index_in_dim(lengths, section, 0, keepdims=False)
    query_rows = queries.reshape(2, 2 * block_len, group_count, group_size, HD)
    stat_shape = (2, 2 * block_len, group_count, group_size)
    start_state = (
        jnp.full(stat_shape, masked_score, jnp.float32),
        jnp.zeros(stat_shape, jnp.float32),
        jnp.zeros(stat_shape + (HD,), jnp.float32),
    )
    state = start_state
    key_piece = lax.all_gather(keys, "cp", axis=0, tiled=True)
    value_piece = lax.all_gather(values, "cp", axis=0, tiled=True)
    shard_count = key_piece.shape[0] // row_count
    first_shard = jnp.int32(0) // row_count
    for base in range(0, shard_count, 4):
        block = min(4, shard_count - base)
        key_block = key_piece[base * row_count : (base + block) * row_count].reshape(
            block, 2, 2 * block_len, group_count, HD
        )
        value_block = value_piece[base * row_count : (base + block) * row_count].reshape(
            block, 2, 2 * block_len, group_count, HD
        )
        shard_ids = first_shard + base + jnp.arange(block, dtype=jnp.int32)
        key_pos = pair_positions(order_row[shard_ids], block_len, cycle_size).reshape(
            block * 2 * block_len
        )
        allowed = jnp.logical_and(
            key_pos[None, None, :] <= query_pos[None, :, None],
            key_pos[None, None, :] < limits[:, None, None],
        )
        allowed = allowed[:, :, None, None, :]
        scores = jnp.einsum(
            "sqgrd,nskgd->sqgrnk", query_rows, key_block, preferred_element_type=jnp.float32
        )
        scores = scores.reshape(stat_shape + (block * 2 * block_len,)) * score_scale
        running_max, running_total, running_sum = state
        block_max = jnp.max(jnp.where(allowed, scores, masked_score), axis=4)
        new_max = jnp.maximum(running_max, block_max)
        weights = jnp.where(allowed, jnp.exp(scores - new_max[..., None]), 0.0)
        carry_factor = jnp.exp(running_max - new_max)
        running_total = running_total * carry_factor + jnp.sum(weights, axis=4)
        shaped = weights.astype(jnp.bfloat16).reshape(stat_shape + (block, 2 * block_len))
        running_sum = running_sum * carry_factor[..., None] + jnp.einsum(
            "sqgrnk,nskgd->sqgrd", shaped, value_block, preferred_element_type=jnp.float32
        )
        state = (new_max, running_total, running_sum)
    attended = (state[2] / state[1][..., None]).astype(jnp.bfloat16).reshape(row_count, width)
    arranged = arrange_rows(attended, routes, section, cycle_size, split_size)
    return shifted(arranged, "pp", 1)


def to_partner(block, mask):
    size = lax.axis_size("cp")
    return lax.ppermute(block, "cp", [(i, i ^ mask) for i in range(size)])


def to_next_section(block, mask):
    sections, size = lax.axis_size("pp"), lax.axis_size("cp")
    route = [
        (p * size + i, ((p + 1) % sections) * size + (i ^ mask))
        for p in range(sections)
        for i in range(size)
    ]
    return lax.ppermute(block, ("pp", "cp"), route)


def row_to_column(row):
    count = row.shape[1]
    down = lax.broadcasted_iota(jnp.int32, (count, count), 0)
    across = lax.broadcasted_iota(jnp.int32, (count, count), 1)
    return jnp.sum(jnp.where(down == across, row, 0), axis=1, keepdims=True)


def rank_in_row(row):
    count = row.shape[1]
    down = lax.broadcasted_iota(jnp.int32, (count, count), 0)
    across = lax.broadcasted_iota(jnp.int32, (count, count), 1)
    hits = jnp.logical_and(row_to_column(row) == row, down < across)
    return jnp.sum(hits.astype(jnp.int32), axis=0, keepdims=True)


def one_hot(rank, match, height):
    ids = lax.broadcasted_iota(jnp.int32, (height, rank.shape[1]), 0)
    return jnp.logical_and(ids == rank, match).astype(jnp.float32).astype(jnp.bfloat16)


def make_ready(keys, values, route_rows, where, *, cycle_size, split_size, packed_rows):
    row_count, width = keys.shape
    sections = route_rows.shape[0]
    head_rows = row_count + 16

    def kernel(where_ref, k_ref, v_ref, r_ref, first_ref, rest_ref, pack_ref):
        section, place = where_ref[0], where_ref[1]
        first_ref[0:row_count, 0:HD] = k_ref[:, 0:HD]
        first_ref[0:row_count, HD : 2 * HD] = v_ref[:, 0:HD]
        spare = jnp.zeros((16 - sections, row_count), jnp.float32)
        sent = jnp.concatenate([r_ref[...].astype(jnp.float32), spare], axis=0).astype(jnp.bfloat16)
        first_ref[row_count:head_rows, 0:HD] = sent
        first_ref[row_count:head_rows, HD : 2 * HD] = jnp.zeros((16, HD), jnp.bfloat16)
        rest_ref[:, 0 : width - HD] = k_ref[:, HD:width]
        rest_ref[:, width - HD :] = v_ref[:, HD:width]
        chips = r_ref[pl.ds(section, 1), :] // split_size
        rank = rank_in_row(chips)
        for mask in range(cycle_size):
            pack_ref[mask] = one_hot(rank, chips == (place ^ mask), packed_rows)

    return pl.pallas_call(
        kernel,
        out_shape=(
            jax.ShapeDtypeStruct((head_rows, 2 * HD), jnp.bfloat16),
            jax.ShapeDtypeStruct((row_count, 2 * (width - HD)), jnp.bfloat16),
            jax.ShapeDtypeStruct((cycle_size, packed_rows, row_count), jnp.bfloat16),
        ),
        in_specs=[pl.BlockSpec(memory_space=pltpu.SMEM)] + [pl.BlockSpec(memory_space=pltpu.VMEM)] * 3,
        name="make_ready",
    )(where, keys, values, route_rows)


def make_unpack(route_rows, heads, where, *, cycle_size, split_size, packed_rows, capacity):
    sections, row_count = route_rows.shape

    def kernel(where_ref, r_ref, *refs):
        head_refs, (own_ref, twin_ref) = refs[: cycle_size - 1], refs[cycle_size - 1 :]
        place, core = where_ref[1], where_ref[2]
        source = (where_ref[0] + sections - 1) % sections
        for mask in range(cycle_size):
            if mask == 0:
                targets = r_ref[pl.ds(source, 1), :]
            else:
                block = head_refs[mask - 1][...].astype(jnp.float32)
                ids = lax.broadcasted_iota(jnp.int32, block.shape, 0)
                targets = jnp.sum(jnp.where(ids == source, block, 0.0), axis=0, keepdims=True)
                targets = targets.astype(jnp.int32)
            chips = targets // split_size
            packed = one_hot(rank_in_row(chips), chips == place, packed_rows)
            slots = rank_in_row(targets)
            for ref, which in ((own_ref, core), (twin_ref, 1 - core)):
                slotted = one_hot(slots, targets == place * split_size + which, capacity)
                ref[mask] = lax.dot_general(
                    slotted, packed, (((1,), (1,)), ((), ())), preferred_element_type=jnp.float32
                ).astype(jnp.bfloat16)

    shape = jax.ShapeDtypeStruct((cycle_size, capacity, packed_rows), jnp.bfloat16)
    return pl.pallas_call(
        kernel,
        grid=(1,),
        out_shape=(shape, shape),
        in_specs=[
            pl.BlockSpec(memory_space=pltpu.SMEM),
            pl.BlockSpec(memory_space=pltpu.VMEM),
        ]
        + [pl.BlockSpec((16, HD), lambda i: (row_count // 16, 0))] * (cycle_size - 1),
        name="make_unpack",
    )(where, route_rows, *heads)


def attend(queries, pieces, pack, pair_order, lengths, where, group, *, cycle_size, group_size):
    row_count = queries.shape[0]
    half = row_count // 2
    block_len = half // 2
    packed_rows = pack.shape[1]
    step_heads = min(4, group_size)
    steps = group_size // step_heads
    tile = step_heads * HD
    scale = HD ** (-0.5)

    def kernel(where_ref, order_ref, len_ref, q_ref, *refs):
        kv_refs, pack_ref, out_refs = refs[: 2 * cycle_size], refs[2 * cycle_size], refs[2 * cycle_size + 1 :]
        section, place = where_ref[0], where_ref[1]
        own = order_ref[section, place]
        row = lax.broadcasted_iota(jnp.int32, (half, cycle_size * half), 0)
        query_pos = jnp.where(row < block_len, own, 2 * cycle_size - 2 - own) * block_len + row
        lane = lax.broadcasted_iota(jnp.int32, (half, half), 1)
        key_pos = []
        for mask in range(cycle_size):
            pair = order_ref[section, place ^ mask]
            key_pos.append(jnp.where(lane < block_len, pair, 2 * cycle_size - 2 - pair) * block_len + lane)
        key_pos = jnp.concatenate(key_pos, axis=1)
        causal = key_pos <= query_pos
        parts = []
        for seq in range(2):
            rows = slice(seq * half, (seq + 1) * half)
            allowed = jnp.logical_and(causal, key_pos < len_ref[section, seq])
            offset = jnp.where(allowed, 0.0, masked_score)
            offset = jnp.concatenate([offset] * step_heads, axis=0)
            k = jnp.concatenate([kv_refs[2 * m][rows, :] for m in range(cycle_size)], axis=0)
            v = jnp.concatenate([kv_refs[2 * m + 1][rows, :] for m in range(cycle_size)], axis=0)
            q = jnp.concatenate([q_ref[rows, h * HD : (h + 1) * HD] for h in range(step_heads)], axis=0)
            scores = lax.dot_general(q, k, (((1,), (1,)), ((), ())), preferred_element_type=jnp.float32)
            scores = jnp.where(offset == 0.0, scores * scale, masked_score)
            weights = jnp.exp(scores - jnp.max(scores, axis=1, keepdims=True))
            total = jnp.sum(weights, axis=1, keepdims=True)
            summed = jnp.dot(weights.astype(jnp.bfloat16), v, preferred_element_type=jnp.float32)
            done = (summed / total).astype(jnp.bfloat16)
            parts.append(
                jnp.concatenate([done[h * half : (h + 1) * half] for h in range(step_heads)], axis=1)
            )
        attended = jnp.concatenate(parts, axis=0)
        for mask in range(cycle_size):
            out_refs[mask][...] = jnp.dot(
                pack_ref[mask], attended, preferred_element_type=jnp.float32
            ).astype(jnp.bfloat16)

    kv_specs, kv_args = [], []
    for key_array, key_col, value_array, value_col in pieces:
        kv_specs.append(pl.BlockSpec((row_count, HD), lambda i, *_, col=key_col: (0, col)))
        kv_specs.append(pl.BlockSpec((row_count, HD), lambda i, *_, col=value_col: (0, col)))
        kv_args += [key_array, value_array]
    return pl.pallas_call(
        kernel,
        grid_spec=pltpu.PrefetchScalarGridSpec(
            num_scalar_prefetch=3,
            grid=(steps,),
            in_specs=[pl.BlockSpec((row_count, tile), lambda i, *_: (0, group * steps + i))]
            + kv_specs
            + [pl.BlockSpec(pack.shape, lambda i, *_: (0, 0, 0))],
            out_specs=[pl.BlockSpec((packed_rows, tile), lambda i, *_: (0, i))] * cycle_size,
        ),
        out_shape=[jax.ShapeDtypeStruct((packed_rows, steps * tile), jnp.bfloat16)] * cycle_size,
        name="attend",
    )(where, pair_order, lengths, queries, *kv_args, pack)


def unpack_rows(received, own_slots, twin_slots, where, out, group, *, group_count, split_size):
    cycle_size, capacity, packed_rows = own_slots.shape
    width = received[0].shape[1]
    tile = min(512, width)
    steps = width // tile
    rows = cycle_size * capacity
    full = split_size * group_count * width

    def kernel(where_ref, *refs):
        in_refs, own_ref, twin_ref = refs[:cycle_size], refs[cycle_size], refs[cycle_size + 1]
        out_ref, send_ref = refs[-2:]
        place = where_ref[1]
        for mask in range(cycle_size):
            block = in_refs[mask][...]
            at = pl.ds(pl.multiple_of((place ^ mask) * capacity, capacity), capacity)
            out_ref[at, :] = jnp.dot(own_ref[mask], block, preferred_element_type=jnp.float32).astype(jnp.bfloat16)
            send_ref[at, :] = jnp.dot(twin_ref[mask], block, preferred_element_type=jnp.float32).astype(jnp.bfloat16)

    slots_spec = pl.BlockSpec(own_slots.shape, lambda i, *_: (0, 0, 0))
    in_specs = [pl.BlockSpec((packed_rows, tile), lambda i, *_: (0, i))] * cycle_size + [slots_spec] * 2
    args = list(received) + [own_slots, twin_slots]
    aliases = {}
    if out is not None:
        in_specs.append(pl.BlockSpec(memory_space=pl.ANY))
        aliases = {len(args) + 1: 0}
        args.append(out)
    return pl.pallas_call(
        kernel,
        grid_spec=pltpu.PrefetchScalarGridSpec(
            num_scalar_prefetch=1,
            grid=(steps,),
            in_specs=in_specs,
            out_specs=[
                pl.BlockSpec((rows, tile), lambda i, w: (0, (w[2] * group_count + group) * steps + i)),
                pl.BlockSpec((rows, tile), lambda i, w: (0, i)),
            ],
        ),
        out_shape=[
            jax.ShapeDtypeStruct((rows, full), jnp.bfloat16),
            jax.ShapeDtypeStruct((rows, width), jnp.bfloat16),
        ],
        input_output_aliases=aliases,
        name="unpack_rows",
    )(where, *args)


def place_twin(block, out, where, group, *, group_count):
    rows, width = block.shape
    tile = min(512, width)
    steps = width // tile

    def kernel(where_ref, in_ref, old_ref, out_ref):
        out_ref[...] = in_ref[...]

    return pl.pallas_call(
        kernel,
        grid_spec=pltpu.PrefetchScalarGridSpec(
            num_scalar_prefetch=1,
            grid=(steps,),
            in_specs=[pl.BlockSpec((rows, tile), lambda i, w: (0, i)), pl.BlockSpec(memory_space=pl.ANY)],
            out_specs=pl.BlockSpec((rows, tile), lambda i, w: (0, ((1 - w[2]) * group_count + group) * steps + i)),
        ),
        out_shape=jax.ShapeDtypeStruct(out.shape, out.dtype),
        input_output_aliases={2: 0},
        name="place_twin",
    )(where, block, out)


def body(queries, keys, values, pair_order, lengths, routes):
    cycle_size = lax.axis_size("cp")
    split_size = lax.axis_size("tp")
    row_count, width = queries.shape
    group_count = keys.shape[1] // HD
    group_size = width // keys.shape[1]
    dest_count = cycle_size * split_size
    capacity = 2 * row_count // dest_count
    packed_rows = min(row_count, split_size * capacity)
    masks = [2, 3, 1, 0]
    where = jnp.stack([lax.axis_index("pp"), lax.axis_index("cp"), lax.axis_index("tp")]).astype(jnp.int32)
    route_rows = routes[:, :, 0]
    head, rest, pack = make_ready(
        keys, values, route_rows, where, cycle_size=cycle_size, split_size=split_size, packed_rows=packed_rows
    )
    heads = {mask: to_partner(head, mask) for mask in masks if mask}
    rests = {mask: to_partner(rest, mask) for mask in masks if mask}
    own_slots, twin_slots = make_unpack(
        route_rows,
        [heads[mask] for mask in range(1, cycle_size)],
        where,
        cycle_size=cycle_size,
        split_size=split_size,
        packed_rows=packed_rows,
        capacity=capacity,
    )
    arrived = []
    for group in range(group_count):
        pieces = [(keys, group, values, group)]
        for mask in range(1, cycle_size):
            if group == 0:
                pieces.append((heads[mask], 0, heads[mask], 1))
            else:
                pieces.append((rests[mask], group - 1, rests[mask], group_count + group - 2))
        packed = attend(
            queries, pieces, pack, pair_order, lengths, where, group, cycle_size=cycle_size, group_size=group_size
        )
        sent = {mask: to_next_section(packed[mask], mask) for mask in masks}
        arrived.append([sent[mask] for mask in range(cycle_size)])
    out = None
    twins = []
    for group in range(group_count):
        out, send = unpack_rows(
            arrived[group], own_slots, twin_slots, where, out, group, group_count=group_count, split_size=split_size
        )
        twins.append(lax.ppermute(send, "tp", [(0, 1), (1, 0)]))
    for group in range(group_count):
        out = place_twin(twins[group], out, where, group, group_count=group_count)
    return out


def solution(mesh):
    placed = (
        P(("pp", "cp"), "tp"),
        P(("pp", "cp"), "tp"),
        P(("pp", "cp"), "tp"),
        P(),
        P(),
        P(None, "cp", None),
    )
    small = mesh.shape["cp"] == 4 and mesh.shape["tp"] == 2
    return jax.shard_map(
        body if small else general_body,
        mesh=mesh,
        in_specs=placed,
        out_specs=P(("pp", "cp", "tp"), None),
        check_vma=False,
    )
```

```python
import jax
import jax.numpy as jnp
from jax import lax
from jax.experimental import pallas as pl
from jax.experimental.pallas import tpu as pltpu
from jax.sharding import PartitionSpec as P

HD = 128


masked_score = -1e30


def shifted(block, axis, distance):
    devices = range(lax.axis_size(axis))
    route = [((i - distance) % len(devices), i) for i in devices]
    return lax.ppermute(block, axis, route)


def pair_positions(pair_ids, block_len, cycle_size):
    offsets = jnp.arange(block_len, dtype=jnp.int32)
    first_half = pair_ids[:, None] * block_len + offsets[None, :]
    second_half = (2 * cycle_size - 1 - pair_ids)[:, None] * block_len + offsets[None, :]
    return jnp.concatenate([first_half, second_half], axis=1)


def dispatch_rows(attended, targets, dest_count, capacity):
    row_count = attended.shape[0]
    matches = targets[:, None] == jnp.arange(dest_count, dtype=jnp.int32)[None, :]
    row_ids = jnp.arange(row_count, dtype=jnp.int32)
    earlier = (row_ids[None, :] < row_ids[:, None]).astype(jnp.bfloat16)
    before = jnp.dot(earlier, matches.astype(jnp.bfloat16), preferred_element_type=jnp.float32)
    slot_index = jnp.sum(jnp.where(matches, before, 0.0), axis=1).astype(jnp.int32)
    slot_ids = jnp.arange(capacity, dtype=jnp.int32)
    picked_rows = jnp.logical_and(
        jnp.transpose(matches)[:, None, :], slot_index[None, None, :] == slot_ids[None, :, None]
    )
    selector = picked_rows.astype(jnp.bfloat16).reshape(dest_count * capacity, row_count)
    return jnp.dot(selector, attended, preferred_element_type=jnp.float32).astype(jnp.bfloat16)


def spread_rows(buffer, cycle_size, split_size, capacity, width):
    flat_buffer = buffer.reshape(cycle_size * split_size, capacity, width)
    moved = lax.all_to_all(flat_buffer, ("cp", "tp"), split_axis=0, concat_axis=0, tiled=True)
    moved = jnp.transpose(moved.reshape(cycle_size, split_size, capacity, width), (0, 2, 1, 3))
    return moved.reshape(cycle_size * capacity, split_size * width)


def arrange_rows(attended, routes, source, cycle_size, split_size):
    row_count, width = attended.shape
    dest_count = cycle_size * split_size
    capacity = 2 * row_count // dest_count
    targets = lax.dynamic_index_in_dim(routes, source, 0, keepdims=False)[:, 0]
    buffer = dispatch_rows(attended, targets, dest_count, capacity)
    buffer = buffer.reshape(cycle_size, split_size, capacity, width)
    return spread_rows(buffer, cycle_size, split_size, capacity, width)


def general_body(queries, keys, values, pair_order, lengths, routes):
    cycle_size = lax.axis_size("cp")
    split_size = lax.axis_size("tp")
    section = lax.axis_index("pp")
    place = lax.axis_index("cp")
    row_count = queries.shape[0]
    block_len = row_count // 4
    width = queries.shape[1]
    group_count = keys.shape[1] // HD
    group_size = width // keys.shape[1]
    score_scale = HD ** (-0.5)
    order_row = lax.dynamic_index_in_dim(pair_order, section, 0, keepdims=False)
    own_pair = lax.dynamic_index_in_dim(order_row, place, 0, keepdims=True)
    query_pos = pair_positions(own_pair, block_len, cycle_size).reshape(2 * block_len)
    limits = lax.dynamic_index_in_dim(lengths, section, 0, keepdims=False)
    query_rows = queries.reshape(2, 2 * block_len, group_count, group_size, HD)
    stat_shape = (2, 2 * block_len, group_count, group_size)
    start_state = (
        jnp.full(stat_shape, masked_score, jnp.float32),
        jnp.zeros(stat_shape, jnp.float32),
        jnp.zeros(stat_shape + (HD,), jnp.float32),
    )
    state = start_state
    key_piece = lax.all_gather(keys, "cp", axis=0, tiled=True)
    value_piece = lax.all_gather(values, "cp", axis=0, tiled=True)
    shard_count = key_piece.shape[0] // row_count
    first_shard = jnp.int32(0) // row_count
    for base in range(0, shard_count, 4):
        block = min(4, shard_count - base)
        key_block = key_piece[base * row_count : (base + block) * row_count].reshape(
            block, 2, 2 * block_len, group_count, HD
        )
        value_block = value_piece[base * row_count : (base + block) * row_count].reshape(
            block, 2, 2 * block_len, group_count, HD
        )
        shard_ids = first_shard + base + jnp.arange(block, dtype=jnp.int32)
        key_pos = pair_positions(order_row[shard_ids], block_len, cycle_size).reshape(
            block * 2 * block_len
        )
        allowed = jnp.logical_and(
            key_pos[None, None, :] <= query_pos[None, :, None],
            key_pos[None, None, :] < limits[:, None, None],
        )
        allowed = allowed[:, :, None, None, :]
        scores = jnp.einsum(
            "sqgrd,nskgd->sqgrnk", query_rows, key_block, preferred_element_type=jnp.float32
        )
        scores = scores.reshape(stat_shape + (block * 2 * block_len,)) * score_scale
        running_max, running_total, running_sum = state
        block_max = jnp.max(jnp.where(allowed, scores, masked_score), axis=4)
        new_max = jnp.maximum(running_max, block_max)
        weights = jnp.where(allowed, jnp.exp(scores - new_max[..., None]), 0.0)
        carry_factor = jnp.exp(running_max - new_max)
        running_total = running_total * carry_factor + jnp.sum(weights, axis=4)
        shaped = weights.astype(jnp.bfloat16).reshape(stat_shape + (block, 2 * block_len))
        running_sum = running_sum * carry_factor[..., None] + jnp.einsum(
            "sqgrnk,nskgd->sqgrd", shaped, value_block, preferred_element_type=jnp.float32
        )
        state = (new_max, running_total, running_sum)
    attended = (state[2] / state[1][..., None]).astype(jnp.bfloat16).reshape(row_count, width)
    arranged = arrange_rows(attended, routes, section, cycle_size, split_size)
    return shifted(arranged, "pp", 1)


def to_partner(block, mask):
    size = lax.axis_size("cp")
    return lax.ppermute(block, "cp", [(i, i ^ mask) for i in range(size)])


def to_next_section(block, mask):
    sections, size = lax.axis_size("pp"), lax.axis_size("cp")
    route = [
        (p * size + i, ((p + 1) % sections) * size + (i ^ mask))
        for p in range(sections)
        for i in range(size)
    ]
    return lax.ppermute(block, ("pp", "cp"), route)


def row_to_column(row):
    count = row.shape[1]
    down = lax.broadcasted_iota(jnp.int32, (count, count), 0)
    across = lax.broadcasted_iota(jnp.int32, (count, count), 1)
    return jnp.sum(jnp.where(down == across, row, 0), axis=1, keepdims=True)


def rank_in_row(row):
    count = row.shape[1]
    down = lax.broadcasted_iota(jnp.int32, (count, count), 0)
    across = lax.broadcasted_iota(jnp.int32, (count, count), 1)
    hits = jnp.logical_and(row_to_column(row) == row, down < across)
    return jnp.sum(hits.astype(jnp.int32), axis=0, keepdims=True)


def one_hot(rank, match, height):
    ids = lax.broadcasted_iota(jnp.int32, (height, rank.shape[1]), 0)
    return jnp.logical_and(ids == rank, match).astype(jnp.float32).astype(jnp.bfloat16)


def in_vmem(array):
    return pltpu.with_memory_space_constraint(array, pltpu.VMEM)


def specs(space, count):
    return [pl.BlockSpec(memory_space=space)] * count


def make_ready(keys, values, pair_order, limits, route_rows, where, *, cycle_size, split_size, packed_rows):
    row_count, width = keys.shape
    sections = route_rows.shape[0]
    half = row_count // 2
    block_len = half // 2
    head_rows = row_count + 16
    total = cycle_size * packed_rows

    def kernel(where_ref, order_ref, limit_ref, k_ref, v_ref, r_ref, first_ref, rest_ref, pack_ref, mask_ref):
        section, place = where_ref[0], where_ref[1]
        first_ref[0:row_count, 0:HD] = k_ref[:, 0:HD]
        first_ref[0:row_count, HD : 2 * HD] = v_ref[:, 0:HD]
        spare = jnp.zeros((16 - sections, row_count), jnp.float32)
        sent = jnp.concatenate([r_ref[...].astype(jnp.float32), spare], axis=0).astype(jnp.bfloat16)
        first_ref[row_count:head_rows, 0:HD] = sent
        first_ref[row_count:head_rows, HD : 2 * HD] = jnp.zeros((16, HD), jnp.bfloat16)
        rest_ref[:, 0 : width - HD] = k_ref[:, HD:width]
        rest_ref[:, width - HD :] = v_ref[:, HD:width]
        chips = r_ref[pl.ds(section, 1), :] // split_size
        rank = rank_in_row(chips)
        none = jnp.zeros((packed_rows, half), jnp.float32)
        for mask in range(cycle_size):
            ids = lax.broadcasted_iota(jnp.int32, (packed_rows, row_count), 0)
            pick = jnp.logical_and(ids == rank, chips == (place ^ mask)).astype(jnp.float32)
            first, second = pick[:, :half], pick[:, half:]
            rows = slice(mask * packed_rows, (mask + 1) * packed_rows)
            later = slice(total + mask * packed_rows, total + (mask + 1) * packed_rows)
            pack_ref[rows, :] = jnp.concatenate([first, none, second, none], axis=1).astype(jnp.bfloat16)
            pack_ref[later, :] = jnp.concatenate([none, first, none, second], axis=1).astype(jnp.bfloat16)
        own = order_ref[section, place]
        lane = lax.broadcasted_iota(jnp.int32, (half, 2 * half), 1) % half
        query_pos = jnp.where(lane < block_len, own, 2 * cycle_size - 2 - own) * block_len + lane
        down = lax.broadcasted_iota(jnp.int32, (half, 2 * half), 0)
        for mask in range(cycle_size):
            pair = order_ref[section, place ^ mask]
            key_pos = jnp.where(down < block_len, pair, 2 * cycle_size - 2 - pair) * block_len + down
            for seq in range(2):
                allowed = jnp.logical_and(key_pos <= query_pos, key_pos < limit_ref[seq, section])
                mask_ref[seq, mask * half : (mask + 1) * half, :] = allowed.astype(jnp.float32)

    return pl.pallas_call(
        kernel,
        out_shape=(
            pltpu.VMEM((head_rows, 2 * HD), jnp.bfloat16),
            pltpu.VMEM((row_count, 2 * (width - HD)), jnp.bfloat16),
            pltpu.VMEM((2 * total, 2 * row_count), jnp.bfloat16),
            pltpu.VMEM((2, cycle_size * half, row_count), jnp.float32),
        ),
        in_specs=specs(pltpu.SMEM, 3) + specs(pltpu.VMEM, 3),
        out_specs=tuple(specs(pltpu.VMEM, 4)),
        name="make_ready",
    )(where, pair_order, limits, keys, values, route_rows)


def make_unpack(route_rows, heads, where, *, cycle_size, split_size, packed_rows, capacity):
    sections, row_count = route_rows.shape
    slot_rows = cycle_size * capacity

    def kernel(where_ref, r_ref, *refs):
        head_refs, slots_ref = refs[: cycle_size - 1], refs[cycle_size - 1]
        place, core = where_ref[1], where_ref[2]
        source = (where_ref[0] + sections - 1) % sections
        slots_ref[...] = jnp.zeros(slots_ref.shape, jnp.bfloat16)
        for mask in range(cycle_size):
            if mask == 0:
                targets = r_ref[pl.ds(source, 1), :]
            else:
                block = head_refs[mask - 1][row_count : row_count + 16, 0:row_count].astype(jnp.float32)
                ids = lax.broadcasted_iota(jnp.int32, block.shape, 0)
                targets = jnp.sum(jnp.where(ids == source, block, 0.0), axis=0, keepdims=True)
                targets = targets.astype(jnp.int32)
            chips = targets // split_size
            packed = one_hot(rank_in_row(chips), chips == place, packed_rows)
            slots = rank_in_row(targets)
            for step, which in enumerate((core, 1 - core)):
                slotted = one_hot(slots, targets == place * split_size + which, capacity)
                at = pl.ds(pl.multiple_of(step * slot_rows + (place ^ mask) * capacity, capacity), capacity)
                slots_ref[at, mask * packed_rows : (mask + 1) * packed_rows] = lax.dot_general(
                    slotted, packed, (((1,), (1,)), ((), ())), preferred_element_type=jnp.float32
                ).astype(jnp.bfloat16)

    return pl.pallas_call(
        kernel,
        out_shape=pltpu.VMEM((split_size * slot_rows, cycle_size * packed_rows), jnp.bfloat16),
        in_specs=specs(pltpu.SMEM, 1) + specs(pltpu.VMEM, cycle_size),
        out_specs=specs(pltpu.VMEM, 1)[0],
        name="make_unpack",
    )(where, route_rows, *[in_vmem(head) for head in heads])


def attend(queries, pieces, pack, allow, group, *, cycle_size, group_size, packed_rows):
    row_count = queries.shape[0]
    half = row_count // 2
    total_rows = cycle_size * packed_rows
    width = group_size * HD
    step_heads = min(4, group_size)
    step_width = step_heads * HD
    steps = group_size // step_heads
    scale = HD ** (-0.5)

    def kernel(q_hbm, pack_ref, allow_ref, *refs):
        kv_refs, out_refs = refs[:cycle_size], refs[cycle_size : 2 * cycle_size]
        q_ref, sems = refs[2 * cycle_size :]
        loads = []
        for step in range(steps):
            at = group * width + step * step_width
            loads.append(
                pltpu.make_async_copy(q_hbm.at[:, at : at + step_width], q_ref.at[step], sems.at[step])
            )
            loads[-1].start()

        def stacked(kind, rows):
            return jnp.concatenate(
                [ref[rows, piece[kind] : piece[kind] + HD] for ref, piece in zip(kv_refs, pieces)], axis=0
            )

        seq_rows = [slice(seq * half, (seq + 1) * half) for seq in range(2)]
        keys = [stacked(1, rows) for rows in seq_rows]
        values = [stacked(2, rows) for rows in seq_rows]
        for step in range(steps):
            loads[step].wait()
            attended = []
            for seq in range(2):
                q = jnp.concatenate(
                    [q_ref[step, seq_rows[seq], h * HD : (h + 1) * HD] for h in range(step_heads)], axis=0
                )
                scores = lax.dot_general(
                    keys[seq], q, (((1,), (1,)), ((), ())), preferred_element_type=jnp.float32
                )
                tiles, totals = [], []
                for pair in range(step_heads // 2):
                    block = scores[:, pair * 2 * half : (pair + 1) * 2 * half] * scale
                    block = jnp.where(allow_ref[seq] > 0.0, block, masked_score)
                    block = jnp.exp(block - jnp.max(block, axis=0, keepdims=True))
                    totals.append(jnp.sum(block, axis=0, keepdims=True))
                    tiles.append(block.astype(jnp.bfloat16))
                weights = jnp.concatenate(tiles, axis=1)
                total = jnp.concatenate(totals, axis=1)
                summed = lax.dot_general(
                    values[seq], weights, (((0,), (0,)), ((), ())), preferred_element_type=jnp.float32
                )
                attended.append((summed / total).astype(jnp.bfloat16))
            for pair in range(step_heads // 2):
                cols = slice(pair * 2 * half, (pair + 1) * 2 * half)
                both = jnp.concatenate([attended[0][:, cols], attended[1][:, cols]], axis=1)
                packed = lax.dot_general(
                    pack_ref[...], both, (((1,), (1,)), ((), ())), preferred_element_type=jnp.float32
                ).astype(jnp.bfloat16)
                for which in range(2):
                    head = step * step_heads + 2 * pair + which
                    for mask in range(cycle_size):
                        at = which * total_rows + mask * packed_rows
                        out_refs[mask][:, head * HD : (head + 1) * HD] = packed[at : at + packed_rows]

    return pl.pallas_call(
        kernel,
        in_specs=specs(pl.ANY, 1) + specs(pltpu.VMEM, 2 + cycle_size),
        out_specs=specs(pltpu.VMEM, cycle_size),
        out_shape=[pltpu.VMEM((packed_rows, width), jnp.bfloat16)] * cycle_size,
        scratch_shapes=[
            pltpu.VMEM((steps, row_count, step_width), jnp.bfloat16),
            pltpu.SemaphoreType.DMA((steps,)),
        ],
        compiler_params=pltpu.CompilerParams(vmem_limit_bytes=32 * 1024 * 1024),
        name="attend",
    )(queries, in_vmem(pack), in_vmem(allow), *[in_vmem(piece[0]) for piece in pieces])


def unpack_rows(received, slots, where, out, group, *, group_count):
    cycle_size = len(received)
    packed_rows, width = received[0].shape
    rows = slots.shape[0] // 2
    full = 2 * group_count * width
    tile = 512

    def kernel(where_ref, *refs):
        in_refs, slots_ref = refs[:cycle_size], refs[cycle_size]
        out_ref, send_ref, own_ref, sems = refs[-4:]
        copies = []
        for step, start in enumerate(range(0, width, tile)):
            cols = slice(start, start + tile)
            block = jnp.concatenate([ref[:, cols] for ref in in_refs], axis=0)
            placed = jnp.dot(slots_ref[...], block, preferred_element_type=jnp.float32).astype(jnp.bfloat16)
            own_ref[:, cols] = placed[:rows]
            send_ref[:, cols] = placed[rows:]
            at = (where_ref[2] * group_count + group) * width + start
            at = pl.ds(pl.multiple_of(at, tile), tile)
            copies.append(pltpu.make_async_copy(own_ref.at[:, cols], out_ref.at[:, at], sems.at[step]))
            copies[-1].start()
        for copy in copies:
            copy.wait()

    in_specs = specs(pltpu.SMEM, 1) + specs(pltpu.VMEM, cycle_size + 1)
    args = [in_vmem(block) for block in received] + [in_vmem(slots)]
    aliases = {}
    if out is not None:
        in_specs += specs(pl.ANY, 1)
        aliases = {len(args) + 1: 0}
        args.append(out)
    return pl.pallas_call(
        kernel,
        in_specs=in_specs,
        out_specs=specs(pl.ANY, 1) + specs(pltpu.VMEM, 1),
        scratch_shapes=[pltpu.VMEM((rows, width), jnp.bfloat16), pltpu.SemaphoreType.DMA((width // tile,))],
        out_shape=[jax.ShapeDtypeStruct((rows, full), jnp.bfloat16), pltpu.VMEM((rows, width), jnp.bfloat16)],
        input_output_aliases=aliases,
        name="unpack_rows",
    )(where, *args)


def place_twins(blocks, out, where):
    count = len(blocks)
    width = blocks[0].shape[1]

    def kernel(where_ref, *refs):
        in_refs, out_ref, sems = refs[:count], refs[-2], refs[-1]
        copies = []
        for group in range(count):
            at = pl.multiple_of(((1 - where_ref[2]) * count + group) * width, width)
            copies.append(
                pltpu.make_async_copy(in_refs[group], out_ref.at[:, pl.ds(at, width)], sems.at[group])
            )
            copies[-1].start()
        for copy in copies:
            copy.wait()

    return pl.pallas_call(
        kernel,
        in_specs=specs(pltpu.SMEM, 1) + specs(pltpu.VMEM, count) + specs(pl.ANY, 1),
        out_specs=specs(pl.ANY, 1)[0],
        scratch_shapes=[pltpu.SemaphoreType.DMA((count,))],
        out_shape=jax.ShapeDtypeStruct(out.shape, out.dtype),
        input_output_aliases={count + 1: 0},
        name="place_twins",
    )(where, *[in_vmem(block) for block in blocks], out)


def body(queries, keys, values, pair_order, lengths, routes):
    cycle_size = lax.axis_size("cp")
    split_size = lax.axis_size("tp")
    row_count, width = queries.shape
    group_count = keys.shape[1] // HD
    group_size = width // keys.shape[1]
    dest_count = cycle_size * split_size
    capacity = 2 * row_count // dest_count
    packed_rows = min(row_count, split_size * capacity)
    masks = [2, 3, 1, 0]
    where = jnp.stack([lax.axis_index("pp"), lax.axis_index("cp"), lax.axis_index("tp")]).astype(jnp.int32)
    route_rows = routes[:, :, 0]
    sizes = dict(cycle_size=cycle_size, split_size=split_size, packed_rows=packed_rows)
    head, rest, pack, allow = make_ready(keys, values, pair_order, lengths.T, route_rows, where, **sizes)
    heads = {mask: to_partner(head, mask) for mask in masks if mask}
    rests = {mask: to_partner(rest, mask) for mask in (2, 1)}
    heads, rests = lax.optimization_barrier((heads, rests))
    rests[3] = to_partner(rests[2], 1)
    slots = make_unpack(route_rows, [heads[mask] for mask in range(1, cycle_size)], where, capacity=capacity, **sizes)
    heads[0], rests[0] = head, rest
    arrived = []
    for group in range(group_count):
        first = (group - 1) * HD
        if group == 0:
            pieces = [(heads[mask], 0, HD) for mask in range(cycle_size)]
        else:
            pieces = [(rests[mask], first, first + keys.shape[1] - HD) for mask in range(cycle_size)]
        packed = attend(
            queries, pieces, pack, allow, group, cycle_size=cycle_size, group_size=group_size, packed_rows=packed_rows
        )
        sent = {mask: to_next_section(packed[mask], mask) for mask in masks}
        arrived.append([sent[mask] for mask in range(cycle_size)])
    out, twins = None, []
    for group in range(group_count):
        out, send = unpack_rows(arrived[group], slots, where, out, group, group_count=group_count)
        twins.append(lax.ppermute(send, "tp", [(0, 1), (1, 0)]))
    return place_twins(twins, out, where)


def solution(mesh):
    placed = (
        P(("pp", "cp"), "tp"),
        P(("pp", "cp"), "tp"),
        P(("pp", "cp"), "tp"),
        P(),
        P(),
        P(None, "cp", None),
    )
    small = mesh.shape["cp"] == 4 and mesh.shape["tp"] == 2
    return jax.shard_map(
        body if small else general_body,
        mesh=mesh,
        in_specs=placed,
        out_specs=P(("pp", "cp", "tp"), None),
        check_vma=False,
    )
```

```python
import jax
import jax.numpy as jnp
from jax import lax
from jax.experimental import pallas as pl
from jax.experimental.pallas import tpu as pltpu
from jax.sharding import PartitionSpec as P

HD = 128


masked_score = -1e30


def shifted(block, axis, distance):
    devices = range(lax.axis_size(axis))
    route = [((i - distance) % len(devices), i) for i in devices]
    return lax.ppermute(block, axis, route)


def pair_positions(pair_ids, block_len, cycle_size):
    offsets = jnp.arange(block_len, dtype=jnp.int32)
    first_half = pair_ids[:, None] * block_len + offsets[None, :]
    second_half = (2 * cycle_size - 1 - pair_ids)[:, None] * block_len + offsets[None, :]
    return jnp.concatenate([first_half, second_half], axis=1)


def dispatch_rows(attended, targets, dest_count, capacity):
    row_count = attended.shape[0]
    matches = targets[:, None] == jnp.arange(dest_count, dtype=jnp.int32)[None, :]
    row_ids = jnp.arange(row_count, dtype=jnp.int32)
    earlier = (row_ids[None, :] < row_ids[:, None]).astype(jnp.bfloat16)
    before = jnp.dot(earlier, matches.astype(jnp.bfloat16), preferred_element_type=jnp.float32)
    slot_index = jnp.sum(jnp.where(matches, before, 0.0), axis=1).astype(jnp.int32)
    slot_ids = jnp.arange(capacity, dtype=jnp.int32)
    picked_rows = jnp.logical_and(
        jnp.transpose(matches)[:, None, :], slot_index[None, None, :] == slot_ids[None, :, None]
    )
    selector = picked_rows.astype(jnp.bfloat16).reshape(dest_count * capacity, row_count)
    return jnp.dot(selector, attended, preferred_element_type=jnp.float32).astype(jnp.bfloat16)


def spread_rows(buffer, cycle_size, split_size, capacity, width):
    flat_buffer = buffer.reshape(cycle_size * split_size, capacity, width)
    moved = lax.all_to_all(flat_buffer, ("cp", "tp"), split_axis=0, concat_axis=0, tiled=True)
    moved = jnp.transpose(moved.reshape(cycle_size, split_size, capacity, width), (0, 2, 1, 3))
    return moved.reshape(cycle_size * capacity, split_size * width)


def arrange_rows(attended, routes, source, cycle_size, split_size):
    row_count, width = attended.shape
    dest_count = cycle_size * split_size
    capacity = 2 * row_count // dest_count
    targets = lax.dynamic_index_in_dim(routes, source, 0, keepdims=False)[:, 0]
    buffer = dispatch_rows(attended, targets, dest_count, capacity)
    buffer = buffer.reshape(cycle_size, split_size, capacity, width)
    return spread_rows(buffer, cycle_size, split_size, capacity, width)


def general_body(queries, keys, values, pair_order, lengths, routes):
    cycle_size = lax.axis_size("cp")
    split_size = lax.axis_size("tp")
    section = lax.axis_index("pp")
    place = lax.axis_index("cp")
    row_count = queries.shape[0]
    block_len = row_count // 4
    width = queries.shape[1]
    group_count = keys.shape[1] // HD
    group_size = width // keys.shape[1]
    score_scale = HD ** (-0.5)
    order_row = lax.dynamic_index_in_dim(pair_order, section, 0, keepdims=False)
    own_pair = lax.dynamic_index_in_dim(order_row, place, 0, keepdims=True)
    query_pos = pair_positions(own_pair, block_len, cycle_size).reshape(2 * block_len)
    limits = lax.dynamic_index_in_dim(lengths, section, 0, keepdims=False)
    query_rows = queries.reshape(2, 2 * block_len, group_count, group_size, HD)
    stat_shape = (2, 2 * block_len, group_count, group_size)
    start_state = (
        jnp.full(stat_shape, masked_score, jnp.float32),
        jnp.zeros(stat_shape, jnp.float32),
        jnp.zeros(stat_shape + (HD,), jnp.float32),
    )
    state = start_state
    key_piece = lax.all_gather(keys, "cp", axis=0, tiled=True)
    value_piece = lax.all_gather(values, "cp", axis=0, tiled=True)
    shard_count = key_piece.shape[0] // row_count
    first_shard = jnp.int32(0) // row_count
    for base in range(0, shard_count, 4):
        block = min(4, shard_count - base)
        key_block = key_piece[base * row_count : (base + block) * row_count].reshape(
            block, 2, 2 * block_len, group_count, HD
        )
        value_block = value_piece[base * row_count : (base + block) * row_count].reshape(
            block, 2, 2 * block_len, group_count, HD
        )
        shard_ids = first_shard + base + jnp.arange(block, dtype=jnp.int32)
        key_pos = pair_positions(order_row[shard_ids], block_len, cycle_size).reshape(
            block * 2 * block_len
        )
        allowed = jnp.logical_and(
            key_pos[None, None, :] <= query_pos[None, :, None],
            key_pos[None, None, :] < limits[:, None, None],
        )
        allowed = allowed[:, :, None, None, :]
        scores = jnp.einsum(
            "sqgrd,nskgd->sqgrnk", query_rows, key_block, preferred_element_type=jnp.float32
        )
        scores = scores.reshape(stat_shape + (block * 2 * block_len,)) * score_scale
        running_max, running_total, running_sum = state
        block_max = jnp.max(jnp.where(allowed, scores, masked_score), axis=4)
        new_max = jnp.maximum(running_max, block_max)
        weights = jnp.where(allowed, jnp.exp(scores - new_max[..., None]), 0.0)
        carry_factor = jnp.exp(running_max - new_max)
        running_total = running_total * carry_factor + jnp.sum(weights, axis=4)
        shaped = weights.astype(jnp.bfloat16).reshape(stat_shape + (block, 2 * block_len))
        running_sum = running_sum * carry_factor[..., None] + jnp.einsum(
            "sqgrnk,nskgd->sqgrd", shaped, value_block, preferred_element_type=jnp.float32
        )
        state = (new_max, running_total, running_sum)
    attended = (state[2] / state[1][..., None]).astype(jnp.bfloat16).reshape(row_count, width)
    arranged = arrange_rows(attended, routes, section, cycle_size, split_size)
    return shifted(arranged, "pp", 1)


def to_partner(block, mask):
    size = lax.axis_size("cp")
    return lax.ppermute(block, "cp", [(i, i ^ mask) for i in range(size)])


def to_next_section(block, mask):
    sections, size = lax.axis_size("pp"), lax.axis_size("cp")
    route = [
        (p * size + i, ((p + 1) % sections) * size + (i ^ mask))
        for p in range(sections)
        for i in range(size)
    ]
    return lax.ppermute(block, ("pp", "cp"), route)


def row_to_column(row):
    count = row.shape[1]
    down = lax.broadcasted_iota(jnp.int32, (count, count), 0)
    across = lax.broadcasted_iota(jnp.int32, (count, count), 1)
    return jnp.sum(jnp.where(down == across, row, 0), axis=1, keepdims=True)


def rank_in_row(row):
    count = row.shape[1]
    down = lax.broadcasted_iota(jnp.int32, (count, count), 0)
    across = lax.broadcasted_iota(jnp.int32, (count, count), 1)
    hits = jnp.logical_and(row_to_column(row) == row, down < across)
    return jnp.sum(hits.astype(jnp.int32), axis=0, keepdims=True)


def one_hot(rank, match, height):
    ids = lax.broadcasted_iota(jnp.int32, (height, rank.shape[1]), 0)
    return jnp.logical_and(ids == rank, match).astype(jnp.float32).astype(jnp.bfloat16)


def in_vmem(array):
    return pltpu.with_memory_space_constraint(array, pltpu.VMEM)


def specs(space, count):
    return [pl.BlockSpec(memory_space=space)] * count


def make_ready(keys, values, pair_order, limits, route_rows, where, *, cycle_size, split_size, packed_rows):
    row_count, width = keys.shape
    sections = route_rows.shape[0]
    half = row_count // 2
    block_len = half // 2
    head_rows = row_count + 16
    total = cycle_size * packed_rows

    def kernel(where_ref, order_ref, limit_ref, k_ref, v_ref, r_ref, first_ref, rest_ref, pack_ref, mask_ref):
        section, place = where_ref[0], where_ref[1]
        first_ref[0:row_count, 0:HD] = k_ref[:, 0:HD]
        first_ref[0:row_count, HD : 2 * HD] = v_ref[:, 0:HD]
        spare = jnp.zeros((16 - sections, row_count), jnp.float32)
        sent = jnp.concatenate([r_ref[...].astype(jnp.float32), spare], axis=0).astype(jnp.bfloat16)
        first_ref[row_count:head_rows, 0:HD] = sent
        first_ref[row_count:head_rows, HD : 2 * HD] = jnp.zeros((16, HD), jnp.bfloat16)
        rest_ref[:, 0 : width - HD] = k_ref[:, HD:width]
        rest_ref[:, width - HD :] = v_ref[:, HD:width]
        chips = r_ref[pl.ds(section, 1), :] // split_size
        rank = rank_in_row(chips)
        none = jnp.zeros((packed_rows, half), jnp.float32)
        for mask in range(cycle_size):
            ids = lax.broadcasted_iota(jnp.int32, (packed_rows, row_count), 0)
            pick = jnp.logical_and(ids == rank, chips == (place ^ mask)).astype(jnp.float32)
            first, second = pick[:, :half], pick[:, half:]
            rows = slice(mask * packed_rows, (mask + 1) * packed_rows)
            later = slice(total + mask * packed_rows, total + (mask + 1) * packed_rows)
            pack_ref[rows, :] = jnp.concatenate([first, none, second, none], axis=1).astype(jnp.bfloat16)
            pack_ref[later, :] = jnp.concatenate([none, first, none, second], axis=1).astype(jnp.bfloat16)
        own = order_ref[section, place]
        lane = lax.broadcasted_iota(jnp.int32, (half, 2 * half), 1) % half
        query_pos = jnp.where(lane < block_len, own, 2 * cycle_size - 2 - own) * block_len + lane
        down = lax.broadcasted_iota(jnp.int32, (half, 2 * half), 0)
        for mask in range(cycle_size):
            pair = order_ref[section, place ^ mask]
            key_pos = jnp.where(down < block_len, pair, 2 * cycle_size - 2 - pair) * block_len + down
            for seq in range(2):
                allowed = jnp.logical_and(key_pos <= query_pos, key_pos < limit_ref[seq, section])
                mask_ref[seq, mask * half : (mask + 1) * half, :] = allowed.astype(jnp.float32)

    return pl.pallas_call(
        kernel,
        out_shape=(
            pltpu.VMEM((head_rows, 2 * HD), jnp.bfloat16),
            pltpu.VMEM((row_count, 2 * (width - HD)), jnp.bfloat16),
            pltpu.VMEM((2 * total, 2 * row_count), jnp.bfloat16),
            pltpu.VMEM((2, cycle_size * half, row_count), jnp.float32),
        ),
        in_specs=specs(pltpu.SMEM, 3) + specs(pltpu.VMEM, 3),
        out_specs=tuple(specs(pltpu.VMEM, 4)),
        name="make_ready",
    )(where, pair_order, limits, keys, values, route_rows)


def make_unpack(route_rows, heads, where, *, cycle_size, split_size, packed_rows, capacity):
    sections, row_count = route_rows.shape
    slot_rows = cycle_size * capacity

    def kernel(where_ref, r_ref, *refs):
        head_refs, slots_ref, most_ref = refs[: cycle_size - 1], refs[cycle_size - 1], refs[cycle_size]
        place, core = where_ref[1], where_ref[2]
        source = (where_ref[0] + sections - 1) % sections
        slots_ref[...] = jnp.zeros(slots_ref.shape, jnp.bfloat16)
        most = jnp.zeros((8, 1), jnp.float32)
        for mask in range(cycle_size):
            if mask == 0:
                targets = r_ref[pl.ds(source, 1), :]
                table = r_ref[...].astype(jnp.float32)
            else:
                block = head_refs[mask - 1][row_count : row_count + 16, 0:row_count].astype(jnp.float32)
                ids = lax.broadcasted_iota(jnp.int32, block.shape, 0)
                targets = jnp.sum(jnp.where(ids == source, block, 0.0), axis=0, keepdims=True)
                targets = targets.astype(jnp.int32)
                table = block[0:sections]
            table = jnp.concatenate([table, jnp.full((8 - sections, row_count), -1.0, jnp.float32)], axis=0)
            for chip in range(cycle_size):
                low = chip * split_size
                hits = jnp.logical_and(table >= low, table < low + split_size).astype(jnp.float32)
                most = jnp.maximum(most, jnp.sum(hits, axis=1, keepdims=True))
            chips = targets // split_size
            packed = one_hot(rank_in_row(chips), chips == place, packed_rows)
            slots = rank_in_row(targets)
            for step, which in enumerate((core, 1 - core)):
                slotted = one_hot(slots, targets == place * split_size + which, capacity)
                at = pl.ds(pl.multiple_of(step * slot_rows + (place ^ mask) * capacity, capacity), capacity)
                slots_ref[at, mask * packed_rows : (mask + 1) * packed_rows] = lax.dot_general(
                    slotted, packed, (((1,), (1,)), ((), ())), preferred_element_type=jnp.float32
                ).astype(jnp.bfloat16)
        most_ref[0] = jnp.max(most).astype(jnp.int32)

    return pl.pallas_call(
        kernel,
        out_shape=(
            pltpu.VMEM((split_size * slot_rows, cycle_size * packed_rows), jnp.bfloat16),
            jax.ShapeDtypeStruct((1,), jnp.int32),
        ),
        in_specs=specs(pltpu.SMEM, 1) + specs(pltpu.VMEM, cycle_size),
        out_specs=(specs(pltpu.VMEM, 1)[0], specs(pltpu.SMEM, 1)[0]),
        name="make_unpack",
    )(where, route_rows, *[in_vmem(head) for head in heads])


def attend(queries, pieces, pack, allow, group, *, cycle_size, group_size, packed_rows):
    row_count = queries.shape[0]
    half = row_count // 2
    total_rows = pack.shape[0] // 2
    stride = total_rows // cycle_size
    width = group_size * HD
    step_heads = min(8, group_size)
    step_width = step_heads * HD
    steps = group_size // step_heads
    scale = HD ** (-0.5)

    def kernel(q_hbm, pack_ref, allow_ref, *refs):
        kv_refs, out_refs = refs[:cycle_size], refs[cycle_size : 2 * cycle_size]
        q_ref, keys_ref, values_ref, sems = refs[2 * cycle_size :]
        for step in range(steps):
            at = group * width + step * step_width
            pltpu.make_async_copy(q_hbm.at[:, at : at + step_width], q_ref.at[step], sems.at[step]).start()

        seq_rows = [slice(seq * half, (seq + 1) * half) for seq in range(2)]
        for seq in range(2):
            for mask, (_, key_col, value_col) in enumerate(pieces):
                at = slice(mask * half, (mask + 1) * half)
                keys_ref[seq, at, :] = kv_refs[mask][seq_rows[seq], key_col : key_col + HD]
                values_ref[seq, :, at] = jnp.transpose(kv_refs[mask][seq_rows[seq], value_col : value_col + HD])

        def advance(step, carry):
            pltpu.make_async_copy(q_hbm.at[:, 0:step_width], q_ref.at[step], sems.at[step]).wait()
            attended = []
            for seq in range(2):
                q = jnp.concatenate(
                    [q_ref[step, seq_rows[seq], h * HD : (h + 1) * HD] for h in range(step_heads)], axis=0
                )
                scores = lax.dot_general(
                    keys_ref[seq], q, (((1,), (1,)), ((), ())), preferred_element_type=jnp.float32
                )
                tiles, totals = [], []
                for pair in range(step_heads // 2):
                    block = scores[:, pair * 2 * half : (pair + 1) * 2 * half] * scale
                    block = jnp.where(allow_ref[seq] > 0.0, block, masked_score)
                    block = jnp.exp(block - jnp.max(block, axis=0, keepdims=True))
                    totals.append(jnp.sum(block, axis=0, keepdims=True))
                    tiles.append(block.astype(jnp.bfloat16))
                weights = jnp.concatenate(tiles, axis=1)
                total = jnp.concatenate(totals, axis=1)
                summed = jnp.dot(values_ref[seq], weights, preferred_element_type=jnp.float32)
                attended.append((summed / total).astype(jnp.bfloat16))
            for pair in range(step_heads // 2):
                cols = slice(pair * 2 * half, (pair + 1) * 2 * half)
                both = jnp.concatenate([attended[0][:, cols], attended[1][:, cols]], axis=1)
                packed = lax.dot_general(
                    pack_ref[...], both, (((1,), (1,)), ((), ())), preferred_element_type=jnp.float32
                ).astype(jnp.bfloat16)
                for which in range(2):
                    head = pl.ds(pl.multiple_of(step * step_width + (2 * pair + which) * HD, HD), HD)
                    for mask in range(cycle_size):
                        at = which * total_rows + mask * stride
                        out_refs[mask][:, head] = packed[at : at + packed_rows]
            return carry

        lax.fori_loop(0, steps, advance, 0)

    return pl.pallas_call(
        kernel,
        in_specs=specs(pltpu.HBM, 1) + specs(pltpu.VMEM, 2 + cycle_size),
        out_specs=specs(pltpu.VMEM, cycle_size),
        out_shape=[pltpu.VMEM((packed_rows, width), jnp.bfloat16)] * cycle_size,
        scratch_shapes=[
            pltpu.VMEM((steps, row_count, step_width), jnp.bfloat16),
            pltpu.VMEM((2, cycle_size * half, HD), jnp.bfloat16),
            pltpu.VMEM((2, HD, cycle_size * half), jnp.bfloat16),
            pltpu.SemaphoreType.DMA((steps,)),
        ],
        compiler_params=pltpu.CompilerParams(vmem_limit_bytes=8 * 1024 * 1024),
        name="attend",
    )(queries, in_vmem(pack), in_vmem(allow), *[in_vmem(piece[0]) for piece in pieces])


def unpack_rows(received, slots, where, out, group, *, group_count):
    cycle_size = len(received)
    packed_rows, width = received[0].shape
    rows = slots.shape[0] // 2
    spare = slots.shape[1] // cycle_size - packed_rows
    full = 2 * group_count * width
    tile = 512

    def kernel(where_ref, *refs):
        in_refs, slots_ref = refs[:cycle_size], refs[cycle_size]
        out_ref, send_ref, own_ref, sems = refs[-4:]
        home = (where_ref[2] * group_count + group) * width

        def copy(step):
            cols = pl.ds(pl.multiple_of(step * tile, tile), tile)
            at = pl.ds(pl.multiple_of(home + step * tile, tile), tile)
            return pltpu.make_async_copy(own_ref.at[:, cols], out_ref.at[:, at], sems.at[step])

        def advance(step, carry):
            cols = pl.ds(pl.multiple_of(step * tile, tile), tile)
            blocks = []
            for ref in in_refs:
                blocks.append(ref[:, cols])
                if spare:
                    blocks.append(jnp.zeros((spare, tile), jnp.bfloat16))
            block = jnp.concatenate(blocks, axis=0)
            placed = jnp.dot(slots_ref[...], block, preferred_element_type=jnp.float32).astype(jnp.bfloat16)
            own_ref[:, cols] = placed[:rows]
            send_ref[:, cols] = placed[rows:]
            copy(step).start()
            return carry

        lax.fori_loop(0, width // tile, advance, 0)
        for step in range(width // tile):
            copy(step).wait()

    in_specs = specs(pltpu.SMEM, 1) + specs(pltpu.VMEM, cycle_size + 1)
    args = [in_vmem(block) for block in received] + [in_vmem(slots)]
    aliases = {}
    if out is not None:
        in_specs += specs(pl.ANY, 1)
        aliases = {len(args) + 1: 0}
        args.append(out)
    return pl.pallas_call(
        kernel,
        in_specs=in_specs,
        out_specs=specs(pl.ANY, 1) + specs(pltpu.VMEM, 1),
        scratch_shapes=[pltpu.VMEM((rows, width), jnp.bfloat16), pltpu.SemaphoreType.DMA((width // tile,))],
        out_shape=[jax.ShapeDtypeStruct((rows, full), jnp.bfloat16), pltpu.VMEM((rows, width), jnp.bfloat16)],
        input_output_aliases=aliases,
        compiler_params=pltpu.CompilerParams(vmem_limit_bytes=8 * 1024 * 1024),
        name="unpack_rows",
    )(where, *args)


def place_twins(blocks, out, where):
    count = len(blocks)
    width = blocks[0].shape[1]

    def kernel(where_ref, *refs):
        in_refs, out_ref, sems = refs[:count], refs[-2], refs[-1]
        copies = []
        for group in range(count):
            at = pl.multiple_of(((1 - where_ref[2]) * count + group) * width, width)
            copies.append(
                pltpu.make_async_copy(in_refs[group], out_ref.at[:, pl.ds(at, width)], sems.at[group])
            )
            copies[-1].start()
        for copy in copies:
            copy.wait()

    return pl.pallas_call(
        kernel,
        in_specs=specs(pltpu.SMEM, 1) + specs(pltpu.VMEM, count) + specs(pl.ANY, 1),
        out_specs=specs(pl.ANY, 1)[0],
        scratch_shapes=[pltpu.SemaphoreType.DMA((count,))],
        out_shape=jax.ShapeDtypeStruct(out.shape, out.dtype),
        input_output_aliases={count + 1: 0},
        compiler_params=pltpu.CompilerParams(vmem_limit_bytes=8 * 1024 * 1024),
        name="place_twins",
    )(where, *[in_vmem(block) for block in blocks], out)


def body(queries, keys, values, pair_order, lengths, routes):
    cycle_size = lax.axis_size("cp")
    split_size = lax.axis_size("tp")
    row_count, width = queries.shape
    group_count = keys.shape[1] // HD
    group_size = width // keys.shape[1]
    dest_count = cycle_size * split_size
    capacity = 2 * row_count // dest_count
    most_rows = min(row_count, split_size * capacity)
    masks = [2, 3, 1, 0]
    where = jnp.stack([lax.axis_index("pp"), lax.axis_index("cp"), lax.axis_index("tp")]).astype(jnp.int32)
    route_rows = routes[:, :, 0]
    sizes = dict(cycle_size=cycle_size, split_size=split_size, packed_rows=most_rows)
    heads_of = dict(cycle_size=cycle_size, group_size=group_size)
    head, rest, pack, allow = make_ready(keys, values, pair_order, lengths.T, route_rows, where, **sizes)
    heads = {mask: to_partner(head, mask) for mask in masks if mask}
    rests = [rest] + [to_partner(rest, mask) for mask in (1, 2)]
    slots, most = make_unpack(
        route_rows, [heads[mask] for mask in range(1, cycle_size)], where, capacity=capacity, **sizes
    )
    heads[0] = head
    pieces = [(heads[mask], 0, HD) for mask in range(cycle_size)]
    leading = attend(queries, pieces, pack, allow, 0, packed_rows=most_rows, **heads_of)

    def deliver(packed_rows, queries, pack, allow, slots, where, rests, leading):
        rests = rests + [to_partner(rests[2], 1)]
        arrived = []
        for group in range(group_count):
            if group == 0:
                packed = [block[:packed_rows] for block in leading]
            else:
                first = (group - 1) * HD
                pieces = [(piece, first, first + keys.shape[1] - HD) for piece in rests]
                packed = attend(queries, pieces, pack, allow, group, packed_rows=packed_rows, **heads_of)
            sent = {mask: to_next_section(packed[mask], mask) for mask in masks}
            arrived.append([sent[mask] for mask in range(cycle_size)])
        out, twins = None, []
        for group in range(group_count):
            out, send = unpack_rows(arrived[group], slots, where, out, group, group_count=group_count)
            twins.append(lax.ppermute(send, "tp", [(0, 1), (1, 0)]))
        return place_twins(twins, out, where)

    heights = [most_rows * 3 // 4, most_rows * 7 // 8, most_rows]
    choice = sum((most[0] > height).astype(jnp.int32) for height in heights[:-1])
    branches = [lambda *args, height=height: deliver(height, *args) for height in heights]
    return lax.switch(choice, branches, queries, pack, allow, slots, where, rests, leading)


def solution(mesh):
    placed = (
        P(("pp", "cp"), "tp"),
        P(("pp", "cp"), "tp"),
        P(("pp", "cp"), "tp"),
        P(),
        P(),
        P(None, "cp", None),
    )
    small = mesh.shape["cp"] == 4 and mesh.shape["tp"] == 2
    return jax.shard_map(
        body if small else general_body,
        mesh=mesh,
        in_specs=placed,
        out_specs=P(("pp", "cp", "tp"), None),
        check_vma=False,
    )
```

```python
import jax
import jax.numpy as jnp
from jax import lax
from jax.experimental import pallas as pl
from jax.experimental.pallas import tpu as pltpu
from jax.sharding import PartitionSpec as P

HD = 128


masked_score = -1e30


def shifted(block, axis, distance):
    devices = range(lax.axis_size(axis))
    route = [((i - distance) % len(devices), i) for i in devices]
    return lax.ppermute(block, axis, route)


def pair_positions(pair_ids, block_len, cycle_size):
    offsets = jnp.arange(block_len, dtype=jnp.int32)
    first_half = pair_ids[:, None] * block_len + offsets[None, :]
    second_half = (2 * cycle_size - 1 - pair_ids)[:, None] * block_len + offsets[None, :]
    return jnp.concatenate([first_half, second_half], axis=1)


def dispatch_rows(attended, targets, dest_count, capacity):
    row_count = attended.shape[0]
    matches = targets[:, None] == jnp.arange(dest_count, dtype=jnp.int32)[None, :]
    row_ids = jnp.arange(row_count, dtype=jnp.int32)
    earlier = (row_ids[None, :] < row_ids[:, None]).astype(jnp.bfloat16)
    before = jnp.dot(earlier, matches.astype(jnp.bfloat16), preferred_element_type=jnp.float32)
    slot_index = jnp.sum(jnp.where(matches, before, 0.0), axis=1).astype(jnp.int32)
    slot_ids = jnp.arange(capacity, dtype=jnp.int32)
    picked_rows = jnp.logical_and(
        jnp.transpose(matches)[:, None, :], slot_index[None, None, :] == slot_ids[None, :, None]
    )
    selector = picked_rows.astype(jnp.bfloat16).reshape(dest_count * capacity, row_count)
    return jnp.dot(selector, attended, preferred_element_type=jnp.float32).astype(jnp.bfloat16)


def spread_rows(buffer, cycle_size, split_size, capacity, width):
    flat_buffer = buffer.reshape(cycle_size * split_size, capacity, width)
    moved = lax.all_to_all(flat_buffer, ("cp", "tp"), split_axis=0, concat_axis=0, tiled=True)
    moved = jnp.transpose(moved.reshape(cycle_size, split_size, capacity, width), (0, 2, 1, 3))
    return moved.reshape(cycle_size * capacity, split_size * width)


def arrange_rows(attended, routes, source, cycle_size, split_size):
    row_count, width = attended.shape
    dest_count = cycle_size * split_size
    capacity = 2 * row_count // dest_count
    targets = lax.dynamic_index_in_dim(routes, source, 0, keepdims=False)[:, 0]
    buffer = dispatch_rows(attended, targets, dest_count, capacity)
    buffer = buffer.reshape(cycle_size, split_size, capacity, width)
    return spread_rows(buffer, cycle_size, split_size, capacity, width)


def general_body(queries, keys, values, pair_order, lengths, routes):
    cycle_size = lax.axis_size("cp")
    split_size = lax.axis_size("tp")
    section = lax.axis_index("pp")
    place = lax.axis_index("cp")
    row_count = queries.shape[0]
    block_len = row_count // 4
    width = queries.shape[1]
    group_count = keys.shape[1] // HD
    group_size = width // keys.shape[1]
    score_scale = HD ** (-0.5)
    order_row = lax.dynamic_index_in_dim(pair_order, section, 0, keepdims=False)
    own_pair = lax.dynamic_index_in_dim(order_row, place, 0, keepdims=True)
    query_pos = pair_positions(own_pair, block_len, cycle_size).reshape(2 * block_len)
    limits = lax.dynamic_index_in_dim(lengths, section, 0, keepdims=False)
    query_rows = queries.reshape(2, 2 * block_len, group_count, group_size, HD)
    stat_shape = (2, 2 * block_len, group_count, group_size)
    start_state = (
        jnp.full(stat_shape, masked_score, jnp.float32),
        jnp.zeros(stat_shape, jnp.float32),
        jnp.zeros(stat_shape + (HD,), jnp.float32),
    )
    state = start_state
    key_piece = lax.all_gather(keys, "cp", axis=0, tiled=True)
    value_piece = lax.all_gather(values, "cp", axis=0, tiled=True)
    shard_count = key_piece.shape[0] // row_count
    first_shard = jnp.int32(0) // row_count
    for base in range(0, shard_count, 4):
        block = min(4, shard_count - base)
        key_block = key_piece[base * row_count : (base + block) * row_count].reshape(
            block, 2, 2 * block_len, group_count, HD
        )
        value_block = value_piece[base * row_count : (base + block) * row_count].reshape(
            block, 2, 2 * block_len, group_count, HD
        )
        shard_ids = first_shard + base + jnp.arange(block, dtype=jnp.int32)
        key_pos = pair_positions(order_row[shard_ids], block_len, cycle_size).reshape(
            block * 2 * block_len
        )
        allowed = jnp.logical_and(
            key_pos[None, None, :] <= query_pos[None, :, None],
            key_pos[None, None, :] < limits[:, None, None],
        )
        allowed = allowed[:, :, None, None, :]
        scores = jnp.einsum(
            "sqgrd,nskgd->sqgrnk", query_rows, key_block, preferred_element_type=jnp.float32
        )
        scores = scores.reshape(stat_shape + (block * 2 * block_len,)) * score_scale
        running_max, running_total, running_sum = state
        block_max = jnp.max(jnp.where(allowed, scores, masked_score), axis=4)
        new_max = jnp.maximum(running_max, block_max)
        weights = jnp.where(allowed, jnp.exp(scores - new_max[..., None]), 0.0)
        carry_factor = jnp.exp(running_max - new_max)
        running_total = running_total * carry_factor + jnp.sum(weights, axis=4)
        shaped = weights.astype(jnp.bfloat16).reshape(stat_shape + (block, 2 * block_len))
        running_sum = running_sum * carry_factor[..., None] + jnp.einsum(
            "sqgrnk,nskgd->sqgrd", shaped, value_block, preferred_element_type=jnp.float32
        )
        state = (new_max, running_total, running_sum)
    attended = (state[2] / state[1][..., None]).astype(jnp.bfloat16).reshape(row_count, width)
    arranged = arrange_rows(attended, routes, section, cycle_size, split_size)
    return shifted(arranged, "pp", 1)


def to_partner(block, mask):
    size = lax.axis_size("cp")
    return lax.ppermute(block, "cp", [(i, i ^ mask) for i in range(size)])


def to_next_section(block, mask):
    sections, size = lax.axis_size("pp"), lax.axis_size("cp")
    route = [
        (p * size + i, ((p + 1) % sections) * size + (i ^ mask))
        for p in range(sections)
        for i in range(size)
    ]
    return lax.ppermute(block, ("pp", "cp"), route)


def row_to_column(row):
    count = row.shape[1]
    down = lax.broadcasted_iota(jnp.int32, (count, count), 0)
    across = lax.broadcasted_iota(jnp.int32, (count, count), 1)
    return jnp.sum(jnp.where(down == across, row, 0), axis=1, keepdims=True)


def rank_in_row(row):
    count = row.shape[1]
    down = lax.broadcasted_iota(jnp.int32, (count, count), 0)
    across = lax.broadcasted_iota(jnp.int32, (count, count), 1)
    hits = jnp.logical_and(row_to_column(row) == row, down < across)
    return jnp.sum(hits.astype(jnp.int32), axis=0, keepdims=True)


def one_hot(rank, match, height):
    ids = lax.broadcasted_iota(jnp.int32, (height, rank.shape[1]), 0)
    return jnp.logical_and(ids == rank, match).astype(jnp.float32).astype(jnp.bfloat16)


def in_vmem(array):
    return pltpu.with_memory_space_constraint(array, pltpu.VMEM)


def specs(space, count):
    return [pl.BlockSpec(memory_space=space)] * count


def make_ready(keys, values, pair_order, limits, route_rows, where, *, cycle_size, split_size, packed_rows):
    row_count, width = keys.shape
    sections = route_rows.shape[0]
    half = row_count // 2
    block_len = half // 2
    head_rows = row_count + 16
    total = cycle_size * packed_rows

    def kernel(where_ref, order_ref, limit_ref, k_ref, v_ref, r_ref, first_ref, rest_ref, pack_ref, mask_ref):
        section, place = where_ref[0], where_ref[1]
        first_ref[0:row_count, 0:HD] = k_ref[:, 0:HD]
        first_ref[0:row_count, HD : 2 * HD] = v_ref[:, 0:HD]
        spare = jnp.zeros((16 - sections, row_count), jnp.float32)
        sent = jnp.concatenate([r_ref[...].astype(jnp.float32), spare], axis=0).astype(jnp.bfloat16)
        first_ref[row_count:head_rows, 0:HD] = sent
        first_ref[row_count:head_rows, HD : 2 * HD] = jnp.zeros((16, HD), jnp.bfloat16)
        rest_ref[:, 0 : width - HD] = k_ref[:, HD:width]
        rest_ref[:, width - HD :] = v_ref[:, HD:width]
        chips = r_ref[pl.ds(section, 1), :] // split_size
        rank = rank_in_row(chips)
        none = jnp.zeros((packed_rows, half), jnp.float32)
        for mask in range(cycle_size):
            ids = lax.broadcasted_iota(jnp.int32, (packed_rows, row_count), 0)
            pick = jnp.logical_and(ids == rank, chips == (place ^ mask)).astype(jnp.float32)
            first, second = pick[:, :half], pick[:, half:]
            rows = slice(mask * packed_rows, (mask + 1) * packed_rows)
            later = slice(total + mask * packed_rows, total + (mask + 1) * packed_rows)
            pack_ref[rows, :] = jnp.concatenate([first, none, second, none], axis=1).astype(jnp.bfloat16)
            pack_ref[later, :] = jnp.concatenate([none, first, none, second], axis=1).astype(jnp.bfloat16)
        own = order_ref[section, place]
        lane = lax.broadcasted_iota(jnp.int32, (half, 2 * half), 1) % half
        query_pos = jnp.where(lane < block_len, own, 2 * cycle_size - 2 - own) * block_len + lane
        down = lax.broadcasted_iota(jnp.int32, (half, 2 * half), 0)
        for mask in range(cycle_size):
            pair = order_ref[section, place ^ mask]
            key_pos = jnp.where(down < block_len, pair, 2 * cycle_size - 2 - pair) * block_len + down
            for seq in range(2):
                allowed = jnp.logical_and(key_pos <= query_pos, key_pos < limit_ref[seq, section])
                mask_ref[seq, mask * half : (mask + 1) * half, :] = allowed.astype(jnp.float32)

    return pl.pallas_call(
        kernel,
        out_shape=(
            pltpu.VMEM((head_rows, 2 * HD), jnp.bfloat16),
            pltpu.VMEM((row_count, 2 * (width - HD)), jnp.bfloat16),
            pltpu.VMEM((2 * total, 2 * row_count), jnp.bfloat16),
            pltpu.VMEM((2, cycle_size * half, row_count), jnp.float32),
        ),
        in_specs=specs(pltpu.SMEM, 3) + specs(pltpu.VMEM, 3),
        out_specs=tuple(specs(pltpu.VMEM, 4)),
        name="make_ready",
    )(where, pair_order, limits, keys, values, route_rows)


def count_rows(route_rows, heads, *, cycle_size, split_size):
    sections, row_count = route_rows.shape

    def kernel(r_ref, *refs):
        head_refs, most_ref = refs[: cycle_size - 1], refs[cycle_size - 1]
        tables = [r_ref[...].astype(jnp.float32)]
        tables += [ref[row_count : row_count + 16, 0:row_count].astype(jnp.float32)[0:sections] for ref in head_refs]
        table = jnp.concatenate(tables, axis=0)
        most = jnp.zeros((sections * cycle_size, 1), jnp.float32)
        for chip in range(cycle_size):
            low = chip * split_size
            hits = jnp.logical_and(table >= low, table < low + split_size).astype(jnp.float32)
            most = jnp.maximum(most, jnp.sum(hits, axis=1, keepdims=True))
        most_ref[0] = jnp.max(most).astype(jnp.int32)

    return pl.pallas_call(
        kernel,
        out_shape=jax.ShapeDtypeStruct((1,), jnp.int32),
        in_specs=specs(pltpu.VMEM, cycle_size),
        out_specs=specs(pltpu.SMEM, 1)[0],
        name="count_rows",
    )(route_rows, *[in_vmem(head) for head in heads])


def make_unpack(route_rows, heads, where, *, cycle_size, split_size, packed_rows, capacity):
    sections, row_count = route_rows.shape
    slot_rows = cycle_size * capacity

    def kernel(where_ref, r_ref, *refs):
        head_refs, slots_ref = refs[: cycle_size - 1], refs[cycle_size - 1]
        place, core = where_ref[1], where_ref[2]
        source = (where_ref[0] + sections - 1) % sections
        slots_ref[...] = jnp.zeros(slots_ref.shape, jnp.bfloat16)
        for mask in range(cycle_size):
            if mask == 0:
                targets = r_ref[pl.ds(source, 1), :]
            else:
                block = head_refs[mask - 1][row_count : row_count + 16, 0:row_count].astype(jnp.float32)
                ids = lax.broadcasted_iota(jnp.int32, block.shape, 0)
                targets = jnp.sum(jnp.where(ids == source, block, 0.0), axis=0, keepdims=True)
                targets = targets.astype(jnp.int32)
            chips = targets // split_size
            packed = one_hot(rank_in_row(chips), chips == place, packed_rows)
            slots = rank_in_row(targets)
            for step, which in enumerate((core, 1 - core)):
                slotted = one_hot(slots, targets == place * split_size + which, capacity)
                at = pl.ds(pl.multiple_of((place ^ mask) * capacity, capacity), capacity)
                slots_ref[step, at, mask * packed_rows : (mask + 1) * packed_rows] = lax.dot_general(
                    slotted, packed, (((1,), (1,)), ((), ())), preferred_element_type=jnp.float32
                ).astype(jnp.bfloat16)

    return pl.pallas_call(
        kernel,
        out_shape=pltpu.VMEM((split_size, slot_rows, cycle_size * packed_rows), jnp.bfloat16),
        in_specs=specs(pltpu.SMEM, 1) + specs(pltpu.VMEM, cycle_size),
        out_specs=specs(pltpu.VMEM, 1)[0],
        name="make_unpack",
    )(where, route_rows, *[in_vmem(head) for head in heads])


def attend(queries, pieces, pack, allow, group, *, cycle_size, group_size, packed_rows):
    row_count = queries.shape[0]
    half = row_count // 2
    total_rows = pack.shape[0] // 2
    stride = total_rows // cycle_size
    width = group_size * HD
    step_heads = min(8, group_size)
    step_width = step_heads * HD
    steps = group_size // step_heads
    scale = HD ** (-0.5)

    def kernel(q_hbm, pack_ref, allow_ref, *refs):
        kv_refs, out_refs = refs[:cycle_size], refs[cycle_size : 2 * cycle_size]
        q_ref, keys_ref, values_ref, sems = refs[2 * cycle_size :]
        for step in range(steps):
            at = group * width + step * step_width
            pltpu.make_async_copy(q_hbm.at[:, at : at + step_width], q_ref.at[step], sems.at[step]).start()

        seq_rows = [slice(seq * half, (seq + 1) * half) for seq in range(2)]
        for seq in range(2):
            for mask, (_, key_col, value_col) in enumerate(pieces):
                at = slice(mask * half, (mask + 1) * half)
                keys_ref[seq, at, :] = kv_refs[mask][seq_rows[seq], key_col : key_col + HD]
                values_ref[seq, :, at] = jnp.transpose(kv_refs[mask][seq_rows[seq], value_col : value_col + HD])

        def advance(step, carry):
            pltpu.make_async_copy(q_hbm.at[:, 0:step_width], q_ref.at[step], sems.at[step]).wait()
            attended = []
            for seq in range(2):
                q = jnp.concatenate(
                    [q_ref[step, seq_rows[seq], h * HD : (h + 1) * HD] for h in range(step_heads)], axis=0
                )
                scores = lax.dot_general(
                    keys_ref[seq], q, (((1,), (1,)), ((), ())), preferred_element_type=jnp.float32
                )
                tiles, totals = [], []
                for pair in range(step_heads // 2):
                    block = scores[:, pair * 2 * half : (pair + 1) * 2 * half] * scale
                    block = jnp.where(allow_ref[seq] > 0.0, block, masked_score)
                    block = jnp.exp(block - jnp.max(block, axis=0, keepdims=True))
                    totals.append(jnp.sum(block, axis=0, keepdims=True))
                    tiles.append(block.astype(jnp.bfloat16))
                weights = jnp.concatenate(tiles, axis=1)
                total = jnp.concatenate(totals, axis=1)
                summed = jnp.dot(values_ref[seq], weights, preferred_element_type=jnp.float32)
                attended.append((summed / total).astype(jnp.bfloat16))
            for pair in range(step_heads // 2):
                cols = slice(pair * 2 * half, (pair + 1) * 2 * half)
                both = jnp.concatenate([attended[0][:, cols], attended[1][:, cols]], axis=1)
                packed = lax.dot_general(
                    pack_ref[...], both, (((1,), (1,)), ((), ())), preferred_element_type=jnp.float32
                ).astype(jnp.bfloat16)
                for which in range(2):
                    head = pl.ds(pl.multiple_of(step * step_width + (2 * pair + which) * HD, HD), HD)
                    for mask in range(cycle_size):
                        at = which * total_rows + mask * stride
                        out_refs[mask][:, head] = packed[at : at + packed_rows]
            return carry

        lax.fori_loop(0, steps, advance, 0)

    return pl.pallas_call(
        kernel,
        in_specs=specs(pltpu.HBM, 1) + specs(pltpu.VMEM, 2 + cycle_size),
        out_specs=specs(pltpu.VMEM, cycle_size),
        out_shape=[pltpu.VMEM((packed_rows, width), jnp.bfloat16)] * cycle_size,
        scratch_shapes=[
            pltpu.VMEM((steps, row_count, step_width), jnp.bfloat16),
            pltpu.VMEM((2, cycle_size * half, HD), jnp.bfloat16),
            pltpu.VMEM((2, HD, cycle_size * half), jnp.bfloat16),
            pltpu.SemaphoreType.DMA((steps,)),
        ],
        compiler_params=pltpu.CompilerParams(vmem_limit_bytes=8 * 1024 * 1024),
        cost_estimate=pl.CostEstimate(flops=20000000000, transcendentals=0, bytes_accessed=0) if group == 0 else None,
        name="attend",
    )(queries, in_vmem(pack), in_vmem(allow), *[in_vmem(piece[0]) for piece in pieces])


def unpack_rows(received, slots, where, out, group, twins, *, group_count, own, twin):
    cycle_size = len(received)
    packed_rows, width = received[0].shape
    rows = slots.shape[1]
    spare = slots.shape[2] // cycle_size - packed_rows
    full = 2 * group_count * width
    tile = 512
    steps = width // tile

    def kernel(*refs):
        refs = list(refs)
        where_ref = refs.pop(0) if own else None
        in_refs = [refs.pop(0) for _ in range(cycle_size)]
        slots_ref = refs.pop(0)
        twin_refs = [refs.pop(0) for _ in twins]
        if own and out is not None:
            refs.pop(0)
        out_ref = refs.pop(0) if own else None
        send_ref = refs.pop(0) if twin else None
        own_ref, sems = refs if own else (None, None)

        def columns(which, index, step, size):
            at = (which * group_count + index) * width + step * size
            return pl.ds(pl.multiple_of(at, size), size)

        def copy(step):
            cols = pl.ds(pl.multiple_of(step * tile, tile), tile)
            at = columns(where_ref[2], group, step, tile)
            return pltpu.make_async_copy(own_ref.at[:, cols], out_ref.at[:, at], sems.at[step])

        def copy_twin(index):
            at = columns(1 - where_ref[2], index, 0, width)
            return pltpu.make_async_copy(twin_refs[index], out_ref.at[:, at], sems.at[steps + index])

        def advance(step, carry):
            cols = pl.ds(pl.multiple_of(step * tile, tile), tile)
            blocks = []
            for ref in in_refs:
                blocks.append(ref[:, cols])
                if spare:
                    blocks.append(jnp.zeros((spare, tile), jnp.bfloat16))
            block = jnp.concatenate(blocks, axis=0)
            if own:
                placed = jnp.dot(slots_ref[0], block, preferred_element_type=jnp.float32)
                own_ref[:, cols] = placed.astype(jnp.bfloat16)
                copy(step).start()
            if twin:
                placed = jnp.dot(slots_ref[1], block, preferred_element_type=jnp.float32)
                send_ref[:, cols] = placed.astype(jnp.bfloat16)
            return carry

        for index in range(len(twins)):
            copy_twin(index).start()
        lax.fori_loop(0, steps, advance, 0)
        if own:
            for step in range(steps):
                copy(step).wait()
        for index in range(len(twins)):
            copy_twin(index).wait()

    in_specs, args, aliases, out_specs, out_shape, scratch = [], [], {}, [], [], []
    if own:
        in_specs += specs(pltpu.SMEM, 1)
        args.append(where)
    in_specs += specs(pltpu.VMEM, cycle_size + 1 + len(twins))
    args += [in_vmem(block) for block in list(received) + [slots] + list(twins)]
    if own:
        if out is not None:
            in_specs += specs(pl.ANY, 1)
            aliases = {len(args): 0}
            args.append(out)
        out_specs += specs(pl.ANY, 1)
        out_shape.append(jax.ShapeDtypeStruct((rows, full), jnp.bfloat16))
        scratch = [
            pltpu.VMEM((rows, width), jnp.bfloat16),
            pltpu.SemaphoreType.DMA((steps + len(twins),)),
        ]
    if twin:
        out_specs += specs(pltpu.VMEM, 1)
        out_shape.append(pltpu.VMEM((rows, width), jnp.bfloat16))
    return pl.pallas_call(
        kernel,
        in_specs=in_specs,
        out_specs=out_specs,
        scratch_shapes=scratch,
        out_shape=out_shape,
        input_output_aliases=aliases,
        compiler_params=pltpu.CompilerParams(vmem_limit_bytes=8 * 1024 * 1024),
        name="unpack_rows",
    )(*args)


def place_twin(block, out, where, group, *, group_count):
    width = block.shape[1]

    def kernel(where_ref, in_ref, old_ref, out_ref, sem):
        at = pl.multiple_of(((1 - where_ref[2]) * group_count + group) * width, width)
        copy = pltpu.make_async_copy(in_ref, out_ref.at[:, pl.ds(at, width)], sem)
        copy.start()
        copy.wait()

    return pl.pallas_call(
        kernel,
        in_specs=specs(pltpu.SMEM, 1) + specs(pltpu.VMEM, 1) + specs(pl.ANY, 1),
        out_specs=specs(pl.ANY, 1)[0],
        scratch_shapes=[pltpu.SemaphoreType.DMA(())],
        out_shape=jax.ShapeDtypeStruct(out.shape, out.dtype),
        input_output_aliases={2: 0},
        compiler_params=pltpu.CompilerParams(vmem_limit_bytes=8 * 1024 * 1024),
        name="place_twin",
    )(where, in_vmem(block), out)


def body(queries, keys, values, pair_order, lengths, routes):
    cycle_size = lax.axis_size("cp")
    split_size = lax.axis_size("tp")
    row_count, width = queries.shape
    group_count = keys.shape[1] // HD
    group_size = width // keys.shape[1]
    dest_count = cycle_size * split_size
    capacity = 2 * row_count // dest_count
    most_rows = min(row_count, split_size * capacity)
    masks = [2, 3, 1, 0]
    where = jnp.stack([lax.axis_index("pp"), lax.axis_index("cp"), lax.axis_index("tp")]).astype(jnp.int32)
    route_rows = routes[:, :, 0]
    sizes = dict(cycle_size=cycle_size, split_size=split_size, packed_rows=most_rows)
    heads_of = dict(cycle_size=cycle_size, group_size=group_size)
    head, rest, pack, allow = make_ready(keys, values, pair_order, lengths.T, route_rows, where, **sizes)
    heads = [head] + [to_partner(head, mask) for mask in range(1, cycle_size)]
    rests = [rest] + [to_partner(rest, mask) for mask in (1, 2)]
    most = count_rows(route_rows, heads[1:], cycle_size=cycle_size, split_size=split_size)
    pieces = [(piece, 0, HD) for piece in heads]
    leading = attend(queries, pieces, pack, allow, 0, packed_rows=most_rows, **heads_of)

    def deliver(packed_rows, queries, pack, allow, route_rows, where, heads, rests, leading):
        rests = rests + [to_partner(rests[2], 1)]
        arrived = []
        for group in range(group_count):
            if group == 0:
                packed = [block[:packed_rows] for block in leading]
            else:
                first = (group - 1) * HD
                pieces = [(piece, first, first + keys.shape[1] - HD) for piece in rests]
                packed = attend(queries, pieces, pack, allow, group, packed_rows=packed_rows, **heads_of)
            sent = {mask: to_next_section(packed[mask], mask) for mask in masks}
            arrived.append([sent[mask] for mask in range(cycle_size)])
        slots = make_unpack(route_rows, heads, where, capacity=capacity, **sizes)
        out, twins = None, []
        swap = [(0, 1), (1, 0)]
        for group in range(group_count - 1):
            out, send = unpack_rows(
                arrived[group], slots, where, out, group, [], group_count=group_count, own=True, twin=True
            )
            twins.append(lax.ppermute(send, "tp", swap))
        last = group_count - 1
        (send,) = unpack_rows(
            arrived[last], slots, where, None, last, [], group_count=group_count, own=False, twin=True
        )
        late = lax.ppermute(send, "tp", swap)
        (out,) = unpack_rows(
            arrived[last], slots, where, out, last, twins, group_count=group_count, own=True, twin=False
        )
        return place_twin(late, out, where, last, group_count=group_count)

    heights = [most_rows * 3 // 4, most_rows * 7 // 8, most_rows]
    choice = sum((most[0] > height).astype(jnp.int32) for height in heights[:-1])
    branches = [lambda *args, height=height: deliver(height, *args) for height in heights]
    return lax.switch(choice, branches, queries, pack, allow, route_rows, where, heads[1:], rests, leading)


def solution(mesh):
    placed = (
        P(("pp", "cp"), "tp"),
        P(("pp", "cp"), "tp"),
        P(("pp", "cp"), "tp"),
        P(),
        P(),
        P(None, "cp", None),
    )
    small = mesh.shape["cp"] == 4 and mesh.shape["tp"] == 2
    return jax.shard_map(
        body if small else general_body,
        mesh=mesh,
        in_specs=placed,
        out_specs=P(("pp", "cp", "tp"), None),
        check_vma=False,
    )
```

```python
import jax
import jax.numpy as jnp
from jax import lax
from jax.experimental import pallas as pl
from jax.experimental.pallas import tpu as pltpu
from jax.sharding import PartitionSpec as P

HD = 128


masked_score = -1e30

STEP_HEADS = 8


def shifted(block, axis, distance):
    devices = range(lax.axis_size(axis))
    route = [((i - distance) % len(devices), i) for i in devices]
    return lax.ppermute(block, axis, route)


def pair_positions(pair_ids, block_len, cycle_size):
    offsets = jnp.arange(block_len, dtype=jnp.int32)
    first_half = pair_ids[:, None] * block_len + offsets[None, :]
    second_half = (2 * cycle_size - 1 - pair_ids)[:, None] * block_len + offsets[None, :]
    return jnp.concatenate([first_half, second_half], axis=1)


def dispatch_rows(attended, targets, dest_count, capacity):
    row_count = attended.shape[0]
    matches = targets[:, None] == jnp.arange(dest_count, dtype=jnp.int32)[None, :]
    row_ids = jnp.arange(row_count, dtype=jnp.int32)
    earlier = (row_ids[None, :] < row_ids[:, None]).astype(jnp.bfloat16)
    before = jnp.dot(earlier, matches.astype(jnp.bfloat16), preferred_element_type=jnp.float32)
    slot_index = jnp.sum(jnp.where(matches, before, 0.0), axis=1).astype(jnp.int32)
    slot_ids = jnp.arange(capacity, dtype=jnp.int32)
    picked_rows = jnp.logical_and(
        jnp.transpose(matches)[:, None, :], slot_index[None, None, :] == slot_ids[None, :, None]
    )
    selector = picked_rows.astype(jnp.bfloat16).reshape(dest_count * capacity, row_count)
    return jnp.dot(selector, attended, preferred_element_type=jnp.float32).astype(jnp.bfloat16)


def spread_rows(buffer, cycle_size, split_size, capacity, width):
    flat_buffer = buffer.reshape(cycle_size * split_size, capacity, width)
    moved = lax.all_to_all(flat_buffer, ("cp", "tp"), split_axis=0, concat_axis=0, tiled=True)
    moved = jnp.transpose(moved.reshape(cycle_size, split_size, capacity, width), (0, 2, 1, 3))
    return moved.reshape(cycle_size * capacity, split_size * width)


def arrange_rows(attended, routes, source, cycle_size, split_size):
    row_count, width = attended.shape
    dest_count = cycle_size * split_size
    capacity = 2 * row_count // dest_count
    targets = lax.dynamic_index_in_dim(routes, source, 0, keepdims=False)[:, 0]
    buffer = dispatch_rows(attended, targets, dest_count, capacity)
    buffer = buffer.reshape(cycle_size, split_size, capacity, width)
    return spread_rows(buffer, cycle_size, split_size, capacity, width)


def general_body(queries, keys, values, pair_order, lengths, routes):
    cycle_size = lax.axis_size("cp")
    split_size = lax.axis_size("tp")
    section = lax.axis_index("pp")
    place = lax.axis_index("cp")
    row_count = queries.shape[0]
    block_len = row_count // 4
    width = queries.shape[1]
    group_count = keys.shape[1] // HD
    group_size = width // keys.shape[1]
    score_scale = HD ** (-0.5)
    order_row = lax.dynamic_index_in_dim(pair_order, section, 0, keepdims=False)
    own_pair = lax.dynamic_index_in_dim(order_row, place, 0, keepdims=True)
    query_pos = pair_positions(own_pair, block_len, cycle_size).reshape(2 * block_len)
    limits = lax.dynamic_index_in_dim(lengths, section, 0, keepdims=False)
    query_rows = queries.reshape(2, 2 * block_len, group_count, group_size, HD)
    stat_shape = (2, 2 * block_len, group_count, group_size)
    start_state = (
        jnp.full(stat_shape, masked_score, jnp.float32),
        jnp.zeros(stat_shape, jnp.float32),
        jnp.zeros(stat_shape + (HD,), jnp.float32),
    )
    state = start_state
    key_piece = lax.all_gather(keys, "cp", axis=0, tiled=True)
    value_piece = lax.all_gather(values, "cp", axis=0, tiled=True)
    shard_count = key_piece.shape[0] // row_count
    first_shard = jnp.int32(0) // row_count
    for base in range(0, shard_count, 4):
        block = min(4, shard_count - base)
        key_block = key_piece[base * row_count : (base + block) * row_count].reshape(
            block, 2, 2 * block_len, group_count, HD
        )
        value_block = value_piece[base * row_count : (base + block) * row_count].reshape(
            block, 2, 2 * block_len, group_count, HD
        )
        shard_ids = first_shard + base + jnp.arange(block, dtype=jnp.int32)
        key_pos = pair_positions(order_row[shard_ids], block_len, cycle_size).reshape(
            block * 2 * block_len
        )
        allowed = jnp.logical_and(
            key_pos[None, None, :] <= query_pos[None, :, None],
            key_pos[None, None, :] < limits[:, None, None],
        )
        allowed = allowed[:, :, None, None, :]
        scores = jnp.einsum(
            "sqgrd,nskgd->sqgrnk", query_rows, key_block, preferred_element_type=jnp.float32
        )
        scores = scores.reshape(stat_shape + (block * 2 * block_len,)) * score_scale
        running_max, running_total, running_sum = state
        block_max = jnp.max(jnp.where(allowed, scores, masked_score), axis=4)
        new_max = jnp.maximum(running_max, block_max)
        weights = jnp.where(allowed, jnp.exp(scores - new_max[..., None]), 0.0)
        carry_factor = jnp.exp(running_max - new_max)
        running_total = running_total * carry_factor + jnp.sum(weights, axis=4)
        shaped = weights.astype(jnp.bfloat16).reshape(stat_shape + (block, 2 * block_len))
        running_sum = running_sum * carry_factor[..., None] + jnp.einsum(
            "sqgrnk,nskgd->sqgrd", shaped, value_block, preferred_element_type=jnp.float32
        )
        state = (new_max, running_total, running_sum)
    attended = (state[2] / state[1][..., None]).astype(jnp.bfloat16).reshape(row_count, width)
    arranged = arrange_rows(attended, routes, section, cycle_size, split_size)
    return shifted(arranged, "pp", 1)


def to_partner(block, mask):
    size = lax.axis_size("cp")
    return lax.ppermute(block, "cp", [(i, i ^ mask) for i in range(size)])


def to_next_section(block, mask):
    sections, size = lax.axis_size("pp"), lax.axis_size("cp")
    route = [
        (p * size + i, ((p + 1) % sections) * size + (i ^ mask))
        for p in range(sections)
        for i in range(size)
    ]
    return lax.ppermute(block, ("pp", "cp"), route)


def row_to_column(row):
    count = row.shape[1]
    down = lax.broadcasted_iota(jnp.int32, (count, count), 0)
    across = lax.broadcasted_iota(jnp.int32, (count, count), 1)
    return jnp.sum(jnp.where(down == across, row, 0), axis=1, keepdims=True)


def rank_in_row(row):
    count = row.shape[1]
    down = lax.broadcasted_iota(jnp.int32, (count, count), 0)
    across = lax.broadcasted_iota(jnp.int32, (count, count), 1)
    hits = jnp.logical_and(row_to_column(row) == row, down < across)
    return jnp.sum(hits.astype(jnp.int32), axis=0, keepdims=True)


def one_hot(rank, match, height):
    ids = lax.broadcasted_iota(jnp.int32, (height, rank.shape[1]), 0)
    return jnp.logical_and(ids == rank, match).astype(jnp.float32).astype(jnp.bfloat16)


def in_vmem(array):
    return pltpu.with_memory_space_constraint(array, pltpu.VMEM)


def specs(space, count):
    return [pl.BlockSpec(memory_space=space)] * count


def message_order(cycle_size):
    return [0, 1, 2, 3][:cycle_size]


def piece_order(cycle_size):
    return [0, 3, 1, 2][:cycle_size]


def make_ready(keys, values, pair_order, limits, route_rows, where, *, cycle_size, split_size, packed_rows):
    row_count, width = keys.shape
    sections = route_rows.shape[0]
    half = row_count // 2
    block_len = half // 2
    head_rows = row_count + 16
    total = cycle_size * packed_rows

    def kernel(where_ref, order_ref, limit_ref, k_ref, v_ref, r_ref, first_ref, rest_ref, pack_ref, mask_ref):
        section, place = where_ref[0], where_ref[1]
        first_ref[0:row_count, 0:HD] = k_ref[:, 0:HD]
        first_ref[0:row_count, HD : 2 * HD] = v_ref[:, 0:HD]
        spare = jnp.zeros((16 - sections, row_count), jnp.float32)
        sent = jnp.concatenate([r_ref[...].astype(jnp.float32), spare], axis=0).astype(jnp.bfloat16)
        first_ref[row_count:head_rows, 0:HD] = sent
        first_ref[row_count:head_rows, HD : 2 * HD] = jnp.zeros((16, HD), jnp.bfloat16)
        rest_ref[:, 0 : width - HD] = k_ref[:, HD:width]
        rest_ref[:, width - HD :] = v_ref[:, HD:width]
        chips = r_ref[pl.ds(section, 1), :] // split_size
        rank = rank_in_row(chips)
        none = jnp.zeros((packed_rows, half), jnp.float32)
        for spot, mask in enumerate(message_order(cycle_size)):
            ids = lax.broadcasted_iota(jnp.int32, (packed_rows, row_count), 0)
            pick = jnp.logical_and(ids == rank, chips == (place ^ mask)).astype(jnp.float32)
            first, second = pick[:, :half], pick[:, half:]
            rows = slice(spot * packed_rows, (spot + 1) * packed_rows)
            later = slice(total + spot * packed_rows, total + (spot + 1) * packed_rows)
            pack_ref[rows, :] = jnp.concatenate([first, none, second, none], axis=1).astype(jnp.bfloat16)
            pack_ref[later, :] = jnp.concatenate([none, first, none, second], axis=1).astype(jnp.bfloat16)
        own = order_ref[section, place]
        lane = lax.broadcasted_iota(jnp.int32, (half, 2 * half), 1) % half
        query_pos = jnp.where(lane < block_len, own, 2 * cycle_size - 2 - own) * block_len + lane
        down = lax.broadcasted_iota(jnp.int32, (half, 2 * half), 0)
        for spot, mask in enumerate(piece_order(cycle_size)):
            pair = order_ref[section, place ^ mask]
            key_pos = jnp.where(down < block_len, pair, 2 * cycle_size - 2 - pair) * block_len + down
            for seq in range(2):
                allowed = jnp.logical_and(key_pos <= query_pos, key_pos < limit_ref[seq, section])
                mask_ref[seq, spot * half : (spot + 1) * half, :] = allowed.astype(jnp.float32)

    return pl.pallas_call(
        kernel,
        out_shape=(
            pltpu.VMEM((head_rows, 2 * HD), jnp.bfloat16),
            pltpu.VMEM((row_count, 2 * (width - HD)), jnp.bfloat16),
            pltpu.VMEM((2 * total, 2 * row_count), jnp.bfloat16),
            pltpu.VMEM((2, cycle_size * half, row_count), jnp.float32),
        ),
        in_specs=specs(pltpu.SMEM, 3) + specs(pltpu.VMEM, 3),
        out_specs=tuple(specs(pltpu.VMEM, 4)),
        name="make_ready",
    )(where, pair_order, limits, keys, values, route_rows)


def make_unpack(route_rows, heads, where, *, cycle_size, split_size, packed_rows, capacity):
    sections, row_count = route_rows.shape
    slot_rows = cycle_size * capacity

    def kernel(where_ref, r_ref, *refs):
        head_refs, slots_ref = refs[: cycle_size - 1], refs[cycle_size - 1]
        place, core = where_ref[1], where_ref[2]
        source = (where_ref[0] + sections - 1) % sections
        slots_ref[...] = jnp.zeros(slots_ref.shape, jnp.bfloat16)
        for spot, mask in enumerate(message_order(cycle_size)):
            if mask == 0:
                targets = r_ref[pl.ds(source, 1), :]
            else:
                block = head_refs[mask - 1][row_count : row_count + 16, 0:row_count].astype(jnp.float32)
                ids = lax.broadcasted_iota(jnp.int32, block.shape, 0)
                targets = jnp.sum(jnp.where(ids == source, block, 0.0), axis=0, keepdims=True)
                targets = targets.astype(jnp.int32)
            chips = targets // split_size
            packed = one_hot(rank_in_row(chips), chips == place, packed_rows)
            slots = rank_in_row(targets)
            for step, which in enumerate((core, 1 - core)):
                slotted = one_hot(slots, targets == place * split_size + which, capacity)
                at = pl.ds(pl.multiple_of((place ^ mask) * capacity, capacity), capacity)
                slots_ref[step, at, spot * packed_rows : (spot + 1) * packed_rows] = lax.dot_general(
                    slotted, packed, (((1,), (1,)), ((), ())), preferred_element_type=jnp.float32
                ).astype(jnp.bfloat16)

    return pl.pallas_call(
        kernel,
        out_shape=pltpu.VMEM((split_size, slot_rows, cycle_size * packed_rows), jnp.bfloat16),
        in_specs=specs(pltpu.SMEM, 1) + specs(pltpu.VMEM, cycle_size),
        out_specs=specs(pltpu.VMEM, 1)[0],
        name="make_unpack",
    )(where, route_rows, *[in_vmem(head) for head in heads])


def attend(queries, pieces, pack, allow, first, count, *, cycle_size, group_size, packed_rows, choose=None):
    row_count = queries.shape[0]
    half = row_count // 2
    total_rows = pack.shape[0] // 2
    stride = total_rows // cycle_size
    step_heads = min(STEP_HEADS, group_size)
    step_width = step_heads * HD
    head_steps = group_size // step_heads
    width = count * step_width
    skipped = first % head_steps
    key_heads = (skipped + count - 1) // head_steps + 1
    scale = HD ** (-0.5)

    def kernel(*refs):
        refs = list(refs)
        q_hbm, pack_ref, allow_ref = refs[:3]
        kv_refs = refs[3 : 3 + cycle_size]
        refs = refs[3 + cycle_size :]
        count_refs = (refs.pop(0), kv_refs[1:], refs.pop(0)) if choose else None
        out_refs, refs = refs[:cycle_size], refs[cycle_size:]
        keys_ref, values_ref, q_ref, sem = refs
        at = slice(first * step_width, first * step_width + width)
        load = pltpu.make_async_copy(q_hbm.at[:, at], q_ref, sem)
        load.start()

        seq_rows = [slice(seq * half, (seq + 1) * half) for seq in range(2)]
        for seq in range(2):
            for mask, (_, key_col, value_col) in enumerate(pieces):
                at = slice(mask * half, (mask + 1) * half)
                for head in range(key_heads):
                    key_cols = slice(key_col + head * HD, key_col + (head + 1) * HD)
                    value_cols = slice(value_col + head * HD, value_col + (head + 1) * HD)
                    keys_ref[head, seq, at, :] = kv_refs[mask][seq_rows[seq], key_cols]
                    values_ref[head, seq, :, at] = jnp.transpose(kv_refs[mask][seq_rows[seq], value_cols])

        if choose:
            count_too_low(*count_refs)
        load.wait()

        def advance(step, carry):
            cols = [
                pl.ds(pl.multiple_of(step * step_width + h * HD, HD), HD) for h in range(step_heads)
            ]
            attended = []
            for seq in range(2):
                q = jnp.concatenate([q_ref[seq_rows[seq], col] for col in cols], axis=0)
                scores = lax.dot_general(
                    keys_ref[(step + skipped) // head_steps, seq], q, (((1,), (1,)), ((), ())), preferred_element_type=jnp.float32
                )
                tiles, totals = [], []
                for pair in range(step_heads // 2):
                    block = scores[:, pair * 2 * half : (pair + 1) * 2 * half] * scale
                    block = jnp.where(allow_ref[seq] > 0.0, block, masked_score)
                    block = jnp.exp(block - jnp.max(block, axis=0, keepdims=True))
                    totals.append(jnp.sum(block, axis=0, keepdims=True))
                    tiles.append(block.astype(jnp.bfloat16))
                weights = jnp.concatenate(tiles, axis=1)
                total = jnp.concatenate(totals, axis=1)
                summed = jnp.dot(values_ref[(step + skipped) // head_steps, seq], weights, preferred_element_type=jnp.float32)
                attended.append((summed / total).astype(jnp.bfloat16))
            for pair in range(step_heads // 2):
                tile = slice(pair * 2 * half, (pair + 1) * 2 * half)
                both = jnp.concatenate([attended[0][:, tile], attended[1][:, tile]], axis=1)
                packed = lax.dot_general(
                    pack_ref[...], both, (((1,), (1,)), ((), ())), preferred_element_type=jnp.float32
                ).astype(jnp.bfloat16)
                for which in range(2):
                    head = pl.ds(pl.multiple_of(step * step_width + (2 * pair + which) * HD, HD), HD)
                    for spot in range(cycle_size):
                        at = which * total_rows + spot * stride
                        out_refs[spot][:, head] = packed[at : at + packed_rows]
            return carry

        lax.fori_loop(0, count, advance, 0)

    def count_too_low(routes_ref, head_refs, count_ref):
        sections = routes_ref.shape[0]
        _, heights, cores = choose
        tables = [routes_ref[...].astype(jnp.float32)]
        tables += [ref[row_count : row_count + 16, 0:row_count].astype(jnp.float32)[0:sections] for ref in head_refs]
        table = jnp.concatenate(tables, axis=0)
        most = jnp.zeros((sections * cycle_size, 1), jnp.float32)
        for low in range(0, cycle_size * cores, cores):
            hits = jnp.logical_and(table >= low, table < low + cores).astype(jnp.float32)
            most = jnp.maximum(most, jnp.sum(hits, axis=1, keepdims=True))
        most = jnp.max(most).astype(jnp.int32)
        count_ref[0] = sum((most > height).astype(jnp.int32) for height in heights)

    args = [queries]
    args += [in_vmem(array) for array in [pack, allow] + [piece[0] for piece in pieces]]
    in_specs = specs(pltpu.HBM, 1) + specs(pltpu.VMEM, 2 + cycle_size)
    out_specs, out_shape = specs(pltpu.VMEM, cycle_size), [pltpu.VMEM((packed_rows, width), jnp.bfloat16)] * cycle_size
    scratch = [
        pltpu.VMEM((key_heads, 2, cycle_size * half, HD), jnp.bfloat16),
        pltpu.VMEM((key_heads, 2, HD, cycle_size * half), jnp.bfloat16),
        pltpu.VMEM((row_count, width), jnp.bfloat16),
        pltpu.SemaphoreType.DMA(()),
    ]
    if choose:
        args.append(choose[0])
        in_specs += specs(pltpu.VMEM, 1)
        out_specs = specs(pltpu.SMEM, 1) + out_specs
        out_shape = [jax.ShapeDtypeStruct((1,), jnp.int32)] + out_shape
    estimate = pl.CostEstimate(flops=20000000000, transcendentals=0, bytes_accessed=0) if choose else None
    return pl.pallas_call(
        kernel,
        in_specs=in_specs,
        out_specs=out_specs,
        out_shape=out_shape,
        scratch_shapes=scratch,
        compiler_params=pltpu.CompilerParams(vmem_limit_bytes=8 * 1024 * 1024),
        cost_estimate=estimate,
        name="attend",
    )(*args)


def unpack_rows(received, slots, where, out, first, twins, *, half_width, own, twin):
    cycle_size = len(received)
    packed_rows, width = received[0].shape
    rows = slots.shape[1]
    spare = slots.shape[2] // cycle_size - packed_rows
    full = 2 * half_width
    tile = 512
    steps = width // tile

    def kernel(*refs):
        refs = list(refs)
        where_ref = refs.pop(0) if own else None
        in_refs = [refs.pop(0) for _ in range(cycle_size)]
        slots_ref = refs.pop(0)
        twin_refs = [refs.pop(0) for _ in twins]
        if own and out is not None:
            refs.pop(0)
        out_ref = refs.pop(0) if own else None
        send_ref = refs.pop(0) if twin else None
        own_ref, sems = refs if own else (None, None)

        def columns(which, column, size):
            return pl.ds(pl.multiple_of(which * half_width + column, tile), size)

        def copy(step):
            cols = pl.ds(pl.multiple_of(step * tile, tile), tile)
            at = columns(where_ref[2], first + step * tile, tile)
            return pltpu.make_async_copy(own_ref.at[:, cols], out_ref.at[:, at], sems.at[step])

        def copy_twin(index):
            at = columns(1 - where_ref[2], twins[index][1], twin_refs[index].shape[1])
            return pltpu.make_async_copy(twin_refs[index], out_ref.at[:, at], sems.at[steps + index])

        def advance(step, carry):
            cols = pl.ds(pl.multiple_of(step * tile, tile), tile)
            blocks = []
            for ref in in_refs:
                blocks.append(ref[:, cols])
                if spare:
                    blocks.append(jnp.zeros((spare, tile), jnp.bfloat16))
            block = jnp.concatenate(blocks, axis=0)
            if own:
                placed = jnp.dot(slots_ref[0], block, preferred_element_type=jnp.float32)
                own_ref[:, cols] = placed.astype(jnp.bfloat16)
                copy(step).start()
            if twin:
                placed = jnp.dot(slots_ref[1], block, preferred_element_type=jnp.float32)
                send_ref[:, cols] = placed.astype(jnp.bfloat16)
            return carry

        for index in range(len(twins)):
            copy_twin(index).start()
        lax.fori_loop(0, steps, advance, 0)
        if own:
            for step in range(steps):
                copy(step).wait()
        for index in range(len(twins)):
            copy_twin(index).wait()

    in_specs, args, aliases, out_specs, out_shape, scratch = [], [], {}, [], [], []
    if own:
        in_specs += specs(pltpu.SMEM, 1)
        args.append(where)
    in_specs += specs(pltpu.VMEM, cycle_size + 1 + len(twins))
    args += [in_vmem(block) for block in list(received) + [slots] + [block for block, _ in twins]]
    if own:
        if out is not None:
            in_specs += specs(pl.ANY, 1)
            aliases = {len(args): 0}
            args.append(out)
        out_specs += specs(pl.ANY, 1)
        out_shape.append(jax.ShapeDtypeStruct((rows, full), jnp.bfloat16))
        scratch = [
            pltpu.VMEM((rows, width), jnp.bfloat16),
            pltpu.SemaphoreType.DMA((steps + len(twins),)),
        ]
    if twin:
        out_specs += specs(pltpu.VMEM, 1)
        out_shape.append(pltpu.VMEM((rows, width), jnp.bfloat16))
    return pl.pallas_call(
        kernel,
        in_specs=in_specs,
        out_specs=out_specs,
        scratch_shapes=scratch,
        out_shape=out_shape,
        input_output_aliases=aliases,
        compiler_params=pltpu.CompilerParams(vmem_limit_bytes=8 * 1024 * 1024),
        name="unpack_rows",
    )(*args)


def place_twin(block, out, where, first, *, half_width):
    width = block.shape[1]

    def kernel(where_ref, in_ref, old_ref, out_ref, sem):
        at = pl.multiple_of((1 - where_ref[2]) * half_width + first, HD)
        copy = pltpu.make_async_copy(in_ref, out_ref.at[:, pl.ds(at, width)], sem)
        copy.start()
        copy.wait()

    return pl.pallas_call(
        kernel,
        in_specs=specs(pltpu.SMEM, 1) + specs(pltpu.VMEM, 1) + specs(pl.ANY, 1),
        out_specs=specs(pl.ANY, 1)[0],
        scratch_shapes=[pltpu.SemaphoreType.DMA(())],
        out_shape=jax.ShapeDtypeStruct(out.shape, out.dtype),
        input_output_aliases={2: 0},
        compiler_params=pltpu.CompilerParams(vmem_limit_bytes=8 * 1024 * 1024),
        name="place_twin",
    )(where, in_vmem(block), out)


def body(queries, keys, values, pair_order, lengths, routes):
    cycle_size = lax.axis_size("cp")
    split_size = lax.axis_size("tp")
    row_count, width = queries.shape
    group_count = keys.shape[1] // HD
    group_size = width // keys.shape[1]
    dest_count = cycle_size * split_size
    capacity = 2 * row_count // dest_count
    most_rows = min(row_count, split_size * capacity)
    where = jnp.stack([lax.axis_index("pp"), lax.axis_index("cp"), lax.axis_index("tp")]).astype(jnp.int32)
    route_rows = routes[:, :, 0]
    sizes = dict(cycle_size=cycle_size, split_size=split_size, packed_rows=most_rows)
    heads_of = dict(cycle_size=cycle_size, group_size=group_size)
    head, rest, pack, allow = make_ready(keys, values, pair_order, lengths.T, route_rows, where, **sizes)
    head_steps = group_size // min(STEP_HEADS, group_size)
    counts = [head_steps] * group_count
    chunks = [(sum(counts[:at]), count) for at, count in enumerate(counts)]
    heads = {mask: to_partner(head, mask) for mask in range(1, cycle_size)}
    heads[0] = head
    rests = [rest] + [to_partner(rest, mask) for mask in (1, 2)]
    heights = [most_rows * 3 // 4, most_rows * 7 // 8, most_rows]
    choice, *leading = attend(
        queries,
        [(heads[mask], 0, HD) for mask in piece_order(cycle_size)],
        pack,
        allow,
        *chunks[0],
        packed_rows=most_rows,
        choose=(route_rows, heights[:-1], split_size),
        **heads_of,
    )
    heads = [heads[mask] for mask in range(1, cycle_size)]
    def deliver(packed_rows, queries, pack, allow, route_rows, where, head, heads, rests, leading):
        rests = rests + [to_partner(rests[2], 1)]
        arrived = []
        every = [head] + list(heads)
        for first, count in chunks:
            if first == 0:
                packed = [block[:packed_rows] for block in leading]
            else:
                key_col = (first // head_steps - 1) * HD
                value_col = key_col + keys.shape[1] - HD
                pieces = [(rests[mask], key_col, value_col) for mask in piece_order(cycle_size)]
                if first < head_steps:
                    pieces = [(every[mask], 0, HD) for mask in piece_order(cycle_size)]
                packed = attend(queries, pieces, pack, allow, first, count, packed_rows=packed_rows, **heads_of)
            arrived.append([to_next_section(*sent) for sent in zip(packed, message_order(cycle_size))])
        slots = make_unpack(route_rows, heads, where, capacity=capacity, **sizes)
        out, twins = None, []
        swap = [(0, 1), (1, 0)]
        starts = [first * width // (group_count * head_steps) for first, _ in chunks]
        for received, column in list(zip(arrived, starts))[:-1]:
            out, send = unpack_rows(
                received, slots, where, out, column, [], half_width=width, own=True, twin=True
            )
            twins.append((lax.ppermute(send, "tp", swap), column))
        (send,) = unpack_rows(
            arrived[-1], slots, where, None, starts[-1], [], half_width=width, own=False, twin=True
        )
        late = lax.ppermute(send, "tp", swap)
        (out,) = unpack_rows(
            arrived[-1], slots, where, out, starts[-1], twins, half_width=width, own=True, twin=False
        )
        return place_twin(late, out, where, starts[-1], half_width=width)

    branches = [lambda *args, height=height: deliver(height, *args) for height in heights]
    return lax.switch(choice[0], branches, queries, pack, allow, route_rows, where, head, heads, rests, leading)


def solution(mesh):
    placed = (
        P(("pp", "cp"), "tp"),
        P(("pp", "cp"), "tp"),
        P(("pp", "cp"), "tp"),
        P(),
        P(),
        P(None, "cp", None),
    )
    small = mesh.shape["cp"] == 4 and mesh.shape["tp"] == 2
    return jax.shard_map(
        body if small else general_body,
        mesh=mesh,
        in_specs=placed,
        out_specs=P(("pp", "cp", "tp"), None),
        check_vma=False,
    )
```

```python
import jax
import jax.numpy as jnp
from jax import lax
from jax.experimental import pallas as pl
from jax.experimental.pallas import tpu as pltpu
from jax.sharding import PartitionSpec as P

HD = 128


masked_score = -1e30

STEP_HEADS = 8


def shifted(block, axis, distance):
    devices = range(lax.axis_size(axis))
    route = [((i - distance) % len(devices), i) for i in devices]
    return lax.ppermute(block, axis, route)


def pair_positions(pair_ids, block_len, cycle_size):
    offsets = jnp.arange(block_len, dtype=jnp.int32)
    first_half = pair_ids[:, None] * block_len + offsets[None, :]
    second_half = (2 * cycle_size - 1 - pair_ids)[:, None] * block_len + offsets[None, :]
    return jnp.concatenate([first_half, second_half], axis=1)


def dispatch_rows(attended, targets, dest_count, capacity):
    row_count = attended.shape[0]
    matches = targets[:, None] == jnp.arange(dest_count, dtype=jnp.int32)[None, :]
    row_ids = jnp.arange(row_count, dtype=jnp.int32)
    earlier = (row_ids[None, :] < row_ids[:, None]).astype(jnp.bfloat16)
    before = jnp.dot(earlier, matches.astype(jnp.bfloat16), preferred_element_type=jnp.float32)
    slot_index = jnp.sum(jnp.where(matches, before, 0.0), axis=1).astype(jnp.int32)
    slot_ids = jnp.arange(capacity, dtype=jnp.int32)
    picked_rows = jnp.logical_and(
        jnp.transpose(matches)[:, None, :], slot_index[None, None, :] == slot_ids[None, :, None]
    )
    selector = picked_rows.astype(jnp.bfloat16).reshape(dest_count * capacity, row_count)
    return jnp.dot(selector, attended, preferred_element_type=jnp.float32).astype(jnp.bfloat16)


def spread_rows(buffer, cycle_size, split_size, capacity, width):
    flat_buffer = buffer.reshape(cycle_size * split_size, capacity, width)
    moved = lax.all_to_all(flat_buffer, ("cp", "tp"), split_axis=0, concat_axis=0, tiled=True)
    moved = jnp.transpose(moved.reshape(cycle_size, split_size, capacity, width), (0, 2, 1, 3))
    return moved.reshape(cycle_size * capacity, split_size * width)


def arrange_rows(attended, routes, source, cycle_size, split_size):
    row_count, width = attended.shape
    dest_count = cycle_size * split_size
    capacity = 2 * row_count // dest_count
    targets = lax.dynamic_index_in_dim(routes, source, 0, keepdims=False)[:, 0]
    buffer = dispatch_rows(attended, targets, dest_count, capacity)
    buffer = buffer.reshape(cycle_size, split_size, capacity, width)
    return spread_rows(buffer, cycle_size, split_size, capacity, width)


def general_body(queries, keys, values, pair_order, lengths, routes):
    cycle_size = lax.axis_size("cp")
    split_size = lax.axis_size("tp")
    section = lax.axis_index("pp")
    place = lax.axis_index("cp")
    row_count = queries.shape[0]
    block_len = row_count // 4
    width = queries.shape[1]
    group_count = keys.shape[1] // HD
    group_size = width // keys.shape[1]
    score_scale = HD ** (-0.5)
    order_row = lax.dynamic_index_in_dim(pair_order, section, 0, keepdims=False)
    own_pair = lax.dynamic_index_in_dim(order_row, place, 0, keepdims=True)
    query_pos = pair_positions(own_pair, block_len, cycle_size).reshape(2 * block_len)
    limits = lax.dynamic_index_in_dim(lengths, section, 0, keepdims=False)
    query_rows = queries.reshape(2, 2 * block_len, group_count, group_size, HD)
    stat_shape = (2, 2 * block_len, group_count, group_size)
    start_state = (
        jnp.full(stat_shape, masked_score, jnp.float32),
        jnp.zeros(stat_shape, jnp.float32),
        jnp.zeros(stat_shape + (HD,), jnp.float32),
    )
    state = start_state
    key_piece = lax.all_gather(keys, "cp", axis=0, tiled=True)
    value_piece = lax.all_gather(values, "cp", axis=0, tiled=True)
    shard_count = key_piece.shape[0] // row_count
    first_shard = jnp.int32(0) // row_count
    for base in range(0, shard_count, 4):
        block = min(4, shard_count - base)
        key_block = key_piece[base * row_count : (base + block) * row_count].reshape(
            block, 2, 2 * block_len, group_count, HD
        )
        value_block = value_piece[base * row_count : (base + block) * row_count].reshape(
            block, 2, 2 * block_len, group_count, HD
        )
        shard_ids = first_shard + base + jnp.arange(block, dtype=jnp.int32)
        key_pos = pair_positions(order_row[shard_ids], block_len, cycle_size).reshape(
            block * 2 * block_len
        )
        allowed = jnp.logical_and(
            key_pos[None, None, :] <= query_pos[None, :, None],
            key_pos[None, None, :] < limits[:, None, None],
        )
        allowed = allowed[:, :, None, None, :]
        scores = jnp.einsum(
            "sqgrd,nskgd->sqgrnk", query_rows, key_block, preferred_element_type=jnp.float32
        )
        scores = scores.reshape(stat_shape + (block * 2 * block_len,)) * score_scale
        running_max, running_total, running_sum = state
        block_max = jnp.max(jnp.where(allowed, scores, masked_score), axis=4)
        new_max = jnp.maximum(running_max, block_max)
        weights = jnp.where(allowed, jnp.exp(scores - new_max[..., None]), 0.0)
        carry_factor = jnp.exp(running_max - new_max)
        running_total = running_total * carry_factor + jnp.sum(weights, axis=4)
        shaped = weights.astype(jnp.bfloat16).reshape(stat_shape + (block, 2 * block_len))
        running_sum = running_sum * carry_factor[..., None] + jnp.einsum(
            "sqgrnk,nskgd->sqgrd", shaped, value_block, preferred_element_type=jnp.float32
        )
        state = (new_max, running_total, running_sum)
    attended = (state[2] / state[1][..., None]).astype(jnp.bfloat16).reshape(row_count, width)
    arranged = arrange_rows(attended, routes, section, cycle_size, split_size)
    return shifted(arranged, "pp", 1)


def to_partner(block, mask):
    size = lax.axis_size("cp")
    return lax.ppermute(block, "cp", [(i, i ^ mask) for i in range(size)])


def to_next_section(block, mask):
    sections, size = lax.axis_size("pp"), lax.axis_size("cp")
    route = [
        (p * size + i, ((p + 1) % sections) * size + (i ^ mask))
        for p in range(sections)
        for i in range(size)
    ]
    return lax.ppermute(block, ("pp", "cp"), route)


def row_to_column(row):
    count = row.shape[1]
    down = lax.broadcasted_iota(jnp.int32, (count, count), 0)
    across = lax.broadcasted_iota(jnp.int32, (count, count), 1)
    return jnp.sum(jnp.where(down == across, row, 0), axis=1, keepdims=True)


def rank_in_row(row):
    count = row.shape[1]
    down = lax.broadcasted_iota(jnp.int32, (count, count), 0)
    across = lax.broadcasted_iota(jnp.int32, (count, count), 1)
    hits = jnp.logical_and(row_to_column(row) == row, down < across)
    return jnp.sum(hits.astype(jnp.int32), axis=0, keepdims=True)


def one_hot(rank, match, height):
    ids = lax.broadcasted_iota(jnp.int32, (height, rank.shape[1]), 0)
    return jnp.logical_and(ids == rank, match).astype(jnp.float32).astype(jnp.bfloat16)


def in_vmem(array):
    return pltpu.with_memory_space_constraint(array, pltpu.VMEM)


def specs(space, count):
    return [pl.BlockSpec(memory_space=space)] * count


def message_order(cycle_size):
    return [0, 1, 2, 3][:cycle_size]


def piece_order(cycle_size):
    return [0, 3, 1, 2][:cycle_size]


def make_ready(keys, values, pair_order, limits, route_rows, where, *, cycle_size, split_size, packed_rows):
    row_count, width = keys.shape
    sections = route_rows.shape[0]
    half = row_count // 2
    block_len = half // 2
    head_rows = row_count + 16
    total = cycle_size * packed_rows

    def kernel(where_ref, order_ref, limit_ref, k_ref, v_ref, r_ref, first_ref, rest_ref, pack_ref, mask_ref):
        section, place = where_ref[0], where_ref[1]
        first_ref[0:row_count, 0:HD] = k_ref[:, 0:HD]
        first_ref[0:row_count, HD : 2 * HD] = v_ref[:, 0:HD]
        spare = jnp.zeros((16 - sections, row_count), jnp.float32)
        sent = jnp.concatenate([r_ref[...].astype(jnp.float32), spare], axis=0).astype(jnp.bfloat16)
        first_ref[row_count:head_rows, 0:HD] = sent
        first_ref[row_count:head_rows, HD : 2 * HD] = jnp.zeros((16, HD), jnp.bfloat16)
        rest_ref[:, 0 : width - HD] = k_ref[:, HD:width]
        rest_ref[:, width - HD :] = v_ref[:, HD:width]
        chips = r_ref[pl.ds(section, 1), :] // split_size
        rank = rank_in_row(chips)
        none = jnp.zeros((packed_rows, half), jnp.float32)
        for spot, mask in enumerate(message_order(cycle_size)):
            ids = lax.broadcasted_iota(jnp.int32, (packed_rows, row_count), 0)
            pick = jnp.logical_and(ids == rank, chips == (place ^ mask)).astype(jnp.float32)
            first, second = pick[:, :half], pick[:, half:]
            rows = slice(spot * packed_rows, (spot + 1) * packed_rows)
            later = slice(total + spot * packed_rows, total + (spot + 1) * packed_rows)
            pack_ref[rows, :] = jnp.concatenate([first, none, second, none], axis=1).astype(jnp.bfloat16)
            pack_ref[later, :] = jnp.concatenate([none, first, none, second], axis=1).astype(jnp.bfloat16)
        own = order_ref[section, place]
        lane = lax.broadcasted_iota(jnp.int32, (half, 2 * half), 1) % half
        query_pos = jnp.where(lane < block_len, own, 2 * cycle_size - 2 - own) * block_len + lane
        down = lax.broadcasted_iota(jnp.int32, (half, 2 * half), 0)
        for spot, mask in enumerate(piece_order(cycle_size)):
            pair = order_ref[section, place ^ mask]
            key_pos = jnp.where(down < block_len, pair, 2 * cycle_size - 2 - pair) * block_len + down
            for seq in range(2):
                allowed = jnp.logical_and(key_pos <= query_pos, key_pos < limit_ref[seq, section])
                mask_ref[seq, spot * half : (spot + 1) * half, :] = allowed.astype(jnp.float32)

    return pl.pallas_call(
        kernel,
        out_shape=(
            pltpu.VMEM((head_rows, 2 * HD), jnp.bfloat16),
            pltpu.VMEM((row_count, 2 * (width - HD)), jnp.bfloat16),
            pltpu.VMEM((2 * total, 2 * row_count), jnp.bfloat16),
            pltpu.VMEM((2, cycle_size * half, row_count), jnp.float32),
        ),
        in_specs=specs(pltpu.SMEM, 3) + specs(pltpu.VMEM, 3),
        out_specs=tuple(specs(pltpu.VMEM, 4)),
        name="make_ready",
    )(where, pair_order, limits, keys, values, route_rows)


def make_unpack(route_rows, heads, where, *, cycle_size, split_size, packed_rows, capacity):
    sections, row_count = route_rows.shape
    slot_rows = cycle_size * capacity

    def kernel(where_ref, r_ref, *refs):
        head_refs, slots_ref = refs[: cycle_size - 1], refs[cycle_size - 1]
        place, core = where_ref[1], where_ref[2]
        source = (where_ref[0] + sections - 1) % sections
        slots_ref[...] = jnp.zeros(slots_ref.shape, jnp.bfloat16)
        for spot, mask in enumerate(message_order(cycle_size)):
            if mask == 0:
                targets = r_ref[pl.ds(source, 1), :]
            else:
                block = head_refs[mask - 1][row_count : row_count + 16, 0:row_count].astype(jnp.float32)
                ids = lax.broadcasted_iota(jnp.int32, block.shape, 0)
                targets = jnp.sum(jnp.where(ids == source, block, 0.0), axis=0, keepdims=True)
                targets = targets.astype(jnp.int32)
            chips = targets // split_size
            packed = one_hot(rank_in_row(chips), chips == place, packed_rows)
            slots = rank_in_row(targets)
            for step, which in enumerate((core, 1 - core)):
                slotted = one_hot(slots, targets == place * split_size + which, capacity)
                at = pl.ds(pl.multiple_of((place ^ mask) * capacity, capacity), capacity)
                slots_ref[step, at, spot * packed_rows : (spot + 1) * packed_rows] = lax.dot_general(
                    slotted, packed, (((1,), (1,)), ((), ())), preferred_element_type=jnp.float32
                ).astype(jnp.bfloat16)

    return pl.pallas_call(
        kernel,
        out_shape=pltpu.VMEM((split_size, slot_rows, cycle_size * packed_rows), jnp.bfloat16),
        in_specs=specs(pltpu.SMEM, 1) + specs(pltpu.VMEM, cycle_size),
        out_specs=specs(pltpu.VMEM, 1)[0],
        name="make_unpack",
    )(where, route_rows, *[in_vmem(head) for head in heads])


def attend(queries, pieces, pack, allow, first, count, *, cycle_size, group_size, packed_rows, choose=None):
    row_count = queries.shape[0]
    half = row_count // 2
    total_rows = pack.shape[0] // 2
    stride = total_rows // cycle_size
    step_heads = min(STEP_HEADS, group_size)
    step_width = step_heads * HD
    head_steps = group_size // step_heads
    width = count * step_width
    skipped = first % head_steps
    key_heads = (skipped + count - 1) // head_steps + 1
    scale = HD ** (-0.5)

    def kernel(*refs):
        refs = list(refs)
        q_hbm, pack_ref, allow_ref = refs[:3]
        kv_refs = refs[3 : 3 + cycle_size]
        refs = refs[3 + cycle_size :]
        count_refs = (refs.pop(0), kv_refs[1:], refs.pop(0)) if choose else None
        out_refs, refs = refs[:cycle_size], refs[cycle_size:]
        keys_ref, values_ref, q_ref, sem = refs
        at = slice(first * step_width, first * step_width + width)
        load = pltpu.make_async_copy(q_hbm.at[:, at], q_ref, sem)
        load.start()

        seq_rows = [slice(seq * half, (seq + 1) * half) for seq in range(2)]
        for seq in range(2):
            for mask, (_, key_col, value_col) in enumerate(pieces):
                at = slice(mask * half, (mask + 1) * half)
                for head in range(key_heads):
                    key_cols = slice(key_col + head * HD, key_col + (head + 1) * HD)
                    value_cols = slice(value_col + head * HD, value_col + (head + 1) * HD)
                    keys_ref[head, seq, at, :] = kv_refs[mask][seq_rows[seq], key_cols]
                    values_ref[head, seq, :, at] = jnp.transpose(kv_refs[mask][seq_rows[seq], value_cols])

        if choose:
            count_too_low(*count_refs)
        load.wait()

        def advance(step, carry):
            cols = [
                pl.ds(pl.multiple_of(step * step_width + h * HD, HD), HD) for h in range(step_heads)
            ]
            attended = []
            for seq in range(2):
                q = jnp.concatenate([q_ref[seq_rows[seq], col] for col in cols], axis=0)
                scores = lax.dot_general(
                    keys_ref[(step + skipped) // head_steps, seq], q, (((1,), (1,)), ((), ())), preferred_element_type=jnp.float32
                )
                tiles, totals = [], []
                for pair in range(step_heads // 2):
                    block = scores[:, pair * 2 * half : (pair + 1) * 2 * half] * scale
                    block = jnp.where(allow_ref[seq] > 0.0, block, masked_score)
                    block = jnp.exp(block - jnp.max(block, axis=0, keepdims=True))
                    totals.append(jnp.sum(block, axis=0, keepdims=True))
                    tiles.append(block.astype(jnp.bfloat16))
                weights = jnp.concatenate(tiles, axis=1)
                total = jnp.concatenate(totals, axis=1)
                summed = jnp.dot(values_ref[(step + skipped) // head_steps, seq], weights, preferred_element_type=jnp.float32)
                attended.append((summed / total).astype(jnp.bfloat16))
            for pair in range(step_heads // 2):
                tile = slice(pair * 2 * half, (pair + 1) * 2 * half)
                both = jnp.concatenate([attended[0][:, tile], attended[1][:, tile]], axis=1)
                packed = lax.dot_general(
                    pack_ref[...], both, (((1,), (1,)), ((), ())), preferred_element_type=jnp.float32
                ).astype(jnp.bfloat16)
                for which in range(2):
                    head = pl.ds(pl.multiple_of(step * step_width + (2 * pair + which) * HD, HD), HD)
                    for spot in range(cycle_size):
                        at = which * total_rows + spot * stride
                        out_refs[spot][:, head] = packed[at : at + packed_rows]
            return carry

        lax.fori_loop(0, count, advance, 0)

    def count_too_low(routes_ref, head_refs, count_ref):
        sections = routes_ref.shape[0]
        _, heights, cores = choose
        tables = [routes_ref[...].astype(jnp.float32)]
        tables += [ref[row_count : row_count + 16, 0:row_count].astype(jnp.float32)[0:sections] for ref in head_refs]
        table = jnp.concatenate(tables, axis=0)
        most = jnp.zeros((sections * cycle_size, 1), jnp.float32)
        for low in range(0, cycle_size * cores, cores):
            hits = jnp.logical_and(table >= low, table < low + cores).astype(jnp.float32)
            most = jnp.maximum(most, jnp.sum(hits, axis=1, keepdims=True))
        most = jnp.max(most).astype(jnp.int32)
        count_ref[0] = sum((most > height).astype(jnp.int32) for height in heights)

    args = [queries]
    args += [in_vmem(array) for array in [pack, allow] + [piece[0] for piece in pieces]]
    in_specs = specs(pltpu.HBM, 1) + specs(pltpu.VMEM, 2 + cycle_size)
    out_specs, out_shape = specs(pltpu.VMEM, cycle_size), [pltpu.VMEM((packed_rows, width), jnp.bfloat16)] * cycle_size
    scratch = [
        pltpu.VMEM((key_heads, 2, cycle_size * half, HD), jnp.bfloat16),
        pltpu.VMEM((key_heads, 2, HD, cycle_size * half), jnp.bfloat16),
        pltpu.VMEM((row_count, width), jnp.bfloat16),
        pltpu.SemaphoreType.DMA(()),
    ]
    if choose:
        args.append(choose[0])
        in_specs += specs(pltpu.VMEM, 1)
        out_specs = specs(pltpu.SMEM, 1) + out_specs
        out_shape = [jax.ShapeDtypeStruct((1,), jnp.int32)] + out_shape
    estimate = pl.CostEstimate(flops=20000000000, transcendentals=0, bytes_accessed=0) if choose else None
    return pl.pallas_call(
        kernel,
        in_specs=in_specs,
        out_specs=out_specs,
        out_shape=out_shape,
        scratch_shapes=scratch,
        compiler_params=pltpu.CompilerParams(vmem_limit_bytes=8 * 1024 * 1024),
        cost_estimate=estimate,
        name="attend",
    )(*args)


def unpack_rows(received, slots, where, out, first, twins, *, half_width, own, twin):
    cycle_size = len(received)
    packed_rows, width = received[0].shape
    rows = slots.shape[1]
    spare = slots.shape[2] // cycle_size - packed_rows
    full = 2 * half_width
    tile = 1024
    steps = width // tile

    def kernel(*refs):
        refs = list(refs)
        where_ref = refs.pop(0) if own else None
        in_refs = [refs.pop(0) for _ in range(cycle_size)]
        slots_ref = refs.pop(0)
        twin_refs = [refs.pop(0) for _ in twins]
        if own and out is not None:
            refs.pop(0)
        out_ref = refs.pop(0) if own else None
        send_ref = refs.pop(0) if twin else None
        own_ref, sems = refs if own else (None, None)

        def columns(which, column, size):
            return pl.ds(pl.multiple_of(which * half_width + column, tile), size)

        def copy(step):
            cols = pl.ds(pl.multiple_of(step * tile, tile), tile)
            at = columns(where_ref[2], first + step * tile, tile)
            return pltpu.make_async_copy(own_ref.at[:, cols], out_ref.at[:, at], sems.at[step])

        def copy_twin(index):
            at = columns(1 - where_ref[2], twins[index][1], twin_refs[index].shape[1])
            return pltpu.make_async_copy(twin_refs[index], out_ref.at[:, at], sems.at[steps + index])

        def advance(step, carry):
            cols = pl.ds(pl.multiple_of(step * tile, tile), tile)
            blocks = []
            for ref in in_refs:
                blocks.append(ref[:, cols])
                if spare:
                    blocks.append(jnp.zeros((spare, tile), jnp.bfloat16))
            block = jnp.concatenate(blocks, axis=0)
            if own:
                placed = jnp.dot(slots_ref[0], block, preferred_element_type=jnp.float32)
                own_ref[:, cols] = placed.astype(jnp.bfloat16)
                copy(step).start()
            if twin:
                placed = jnp.dot(slots_ref[1], block, preferred_element_type=jnp.float32)
                send_ref[:, cols] = placed.astype(jnp.bfloat16)
            return carry

        for index in range(len(twins)):
            copy_twin(index).start()
        lax.fori_loop(0, steps, advance, 0)
        if own:
            for step in range(steps):
                copy(step).wait()
        for index in range(len(twins)):
            copy_twin(index).wait()

    in_specs, args, aliases, out_specs, out_shape, scratch = [], [], {}, [], [], []
    if own:
        in_specs += specs(pltpu.SMEM, 1)
        args.append(where)
    in_specs += specs(pltpu.VMEM, cycle_size + 1 + len(twins))
    args += [in_vmem(block) for block in list(received) + [slots] + [block for block, _ in twins]]
    if own:
        if out is not None:
            in_specs += specs(pl.ANY, 1)
            aliases = {len(args): 0}
            args.append(out)
        out_specs += specs(pl.ANY, 1)
        out_shape.append(jax.ShapeDtypeStruct((rows, full), jnp.bfloat16))
        scratch = [
            pltpu.VMEM((rows, width), jnp.bfloat16),
            pltpu.SemaphoreType.DMA((steps + len(twins),)),
        ]
    if twin:
        out_specs += specs(pltpu.VMEM, 1)
        out_shape.append(pltpu.VMEM((rows, width), jnp.bfloat16))
    return pl.pallas_call(
        kernel,
        in_specs=in_specs,
        out_specs=out_specs,
        scratch_shapes=scratch,
        out_shape=out_shape,
        input_output_aliases=aliases,
        compiler_params=pltpu.CompilerParams(vmem_limit_bytes=8 * 1024 * 1024),
        name="unpack_rows",
    )(*args)


def place_twin(block, out, where, first, *, half_width):
    width = block.shape[1]

    def kernel(where_ref, in_ref, old_ref, out_ref, sem):
        at = pl.multiple_of((1 - where_ref[2]) * half_width + first, HD)
        copy = pltpu.make_async_copy(in_ref, out_ref.at[:, pl.ds(at, width)], sem)
        copy.start()
        copy.wait()

    return pl.pallas_call(
        kernel,
        in_specs=specs(pltpu.SMEM, 1) + specs(pltpu.VMEM, 1) + specs(pl.ANY, 1),
        out_specs=specs(pl.ANY, 1)[0],
        scratch_shapes=[pltpu.SemaphoreType.DMA(())],
        out_shape=jax.ShapeDtypeStruct(out.shape, out.dtype),
        input_output_aliases={2: 0},
        compiler_params=pltpu.CompilerParams(vmem_limit_bytes=8 * 1024 * 1024),
        name="place_twin",
    )(where, in_vmem(block), out)


def body(queries, keys, values, pair_order, lengths, routes):
    cycle_size = lax.axis_size("cp")
    split_size = lax.axis_size("tp")
    row_count, width = queries.shape
    group_count = keys.shape[1] // HD
    group_size = width // keys.shape[1]
    dest_count = cycle_size * split_size
    capacity = 2 * row_count // dest_count
    most_rows = min(row_count, split_size * capacity)
    where = jnp.stack([lax.axis_index("pp"), lax.axis_index("cp"), lax.axis_index("tp")]).astype(jnp.int32)
    route_rows = routes[:, :, 0]
    sizes = dict(cycle_size=cycle_size, split_size=split_size, packed_rows=most_rows)
    heads_of = dict(cycle_size=cycle_size, group_size=group_size)
    head, rest, pack, allow = make_ready(keys, values, pair_order, lengths.T, route_rows, where, **sizes)
    head_steps = group_size // min(STEP_HEADS, group_size)
    counts = [head_steps] * group_count
    chunks = [(sum(counts[:at]), count) for at, count in enumerate(counts)]
    heads = {mask: to_partner(head, mask) for mask in range(1, cycle_size)}
    heads[0] = head
    rests = [rest] + [to_partner(rest, mask) for mask in (1, 2)]
    heights = [most_rows * 3 // 4, most_rows * 7 // 8, most_rows]
    choice, *leading = attend(
        queries,
        [(heads[mask], 0, HD) for mask in piece_order(cycle_size)],
        pack,
        allow,
        *chunks[0],
        packed_rows=most_rows,
        choose=(route_rows, heights[:-1], split_size),
        **heads_of,
    )
    heads = [heads[mask] for mask in range(1, cycle_size)]
    def deliver(packed_rows, queries, pack, allow, route_rows, where, head, heads, rests, leading):
        rests = rests + [to_partner(rests[2], 1)]
        arrived = []
        every = [head] + list(heads)
        for first, count in chunks:
            if first == 0:
                packed = [block[:packed_rows] for block in leading]
            else:
                key_col = (first // head_steps - 1) * HD
                value_col = key_col + keys.shape[1] - HD
                pieces = [(rests[mask], key_col, value_col) for mask in piece_order(cycle_size)]
                if first < head_steps:
                    pieces = [(every[mask], 0, HD) for mask in piece_order(cycle_size)]
                packed = attend(queries, pieces, pack, allow, first, count, packed_rows=packed_rows, **heads_of)
            arrived.append([to_next_section(*sent) for sent in zip(packed, message_order(cycle_size))])
        slots = make_unpack(route_rows, heads, where, capacity=capacity, **sizes)
        out, twins = None, []
        swap = [(0, 1), (1, 0)]
        starts = [first * width // (group_count * head_steps) for first, _ in chunks]
        for received, column in list(zip(arrived, starts))[:-1]:
            out, send = unpack_rows(
                received, slots, where, out, column, [], half_width=width, own=True, twin=True
            )
            twins.append((lax.ppermute(send, "tp", swap), column))
        (send,) = unpack_rows(
            arrived[-1], slots, where, None, starts[-1], [], half_width=width, own=False, twin=True
        )
        late = lax.ppermute(send, "tp", swap)
        (out,) = unpack_rows(
            arrived[-1], slots, where, out, starts[-1], twins, half_width=width, own=True, twin=False
        )
        return place_twin(late, out, where, starts[-1], half_width=width)

    branches = [lambda *args, height=height: deliver(height, *args) for height in heights]
    return lax.switch(choice[0], branches, queries, pack, allow, route_rows, where, head, heads, rests, leading)


def solution(mesh):
    placed = (
        P(("pp", "cp"), "tp"),
        P(("pp", "cp"), "tp"),
        P(("pp", "cp"), "tp"),
        P(),
        P(),
        P(None, "cp", None),
    )
    small = mesh.shape["cp"] == 4 and mesh.shape["tp"] == 2
    return jax.shard_map(
        body if small else general_body,
        mesh=mesh,
        in_specs=placed,
        out_specs=P(("pp", "cp", "tp"), None),
        check_vma=False,
    )
```
